32 devices in a mesh: seq: 8 (over y, x, core), head: 4 (over z).
Axes of the slice: x: 2, y: 2, z: 4, core: 2. Of those that a mesh axis runs over, the one named last changes fastest.
Arguments:
- inputs: bfloat16 [2048, 4096], P('seq'), may hold values from -6 to 6
- x_weight: bfloat16 [4096, 8192], P('seq', 'head'), may hold values from -0.125 to 0.125
- b_values: bfloat16 [2048, 8, 128], P('seq'), may hold values from -0.5 to 0.5
- c_values: bfloat16 [2048, 8, 128], P('seq'), may hold values from -0.375 to 0.375
- gate_z: bfloat16 [2048, 8192], P('seq', 'head'), may hold values from -6 to 6
- log_decay: float32 [2048, 128], P('seq', 'head'), may hold values from -2 to 0
- skip_gain: float32 [128], P('head'), may hold values from 0.5 to 1.5
- grad_out: bfloat16 [2048, 8192], P('seq', 'head'), may hold values from -6 to 6
Outputs:
- input_grad: bfloat16 [2048, 4096], P('seq', 'head')
- z_grad: bfloat16 [2048, 8192], P('seq', 'head')
The draws below stay inside these ranges and needn't reach their ends.
All inputs are finite; a program needn't handle non-finite values.
Results may differ from the reference program's by a relative error of at most 0.0095.
Values may be sent and summed in bfloat16 or wider, within the bound.
A program may use at most 128 MiB of HBM per device.

```python
import jax
import jax.numpy as jnp
from jax import lax

D = 4096
HEADS = 128
HEAD_DIM = 64
STATE = 128
GROUPS = 8
SPAN = 256
SEQLEN = 2048
N_HEAD = 4


def draw_log_decay(key, part):
    keys = jax.random.split(jax.random.fold_in(key, 17), 6)
    slow = jax.random.randint(keys[0], (HEADS,), 0, 2) == 1
    slow_rate = jax.random.uniform(keys[1], (HEADS,), jnp.float32, 0.2, 0.6) / SEQLEN
    fast_rate = jax.random.uniform(keys[2], (HEADS,), jnp.float32, 16.0, 24.0) / SPAN
    rates = jnp.where(slow, slow_rate, fast_rate)
    jitter = jax.random.uniform(keys[3], (SEQLEN, HEADS), jnp.float32, 0.5, 1.5)
    spots = jax.random.randint(keys[4], (3,), 0, SEQLEN)
    hits = jnp.sum((jnp.arange(SEQLEN)[:, None] == spots[None, :]).astype(jnp.float32), axis=1)
    hits = jnp.minimum(hits, 1.0)
    losses = jax.random.uniform(keys[5], (SEQLEN, HEADS), jnp.float32, 0.22, 0.51)
    return -(rates[None, :] * jitter + hits[:, None] * losses)


def spiked(drawn, rng, source, target, shards_of, factor):
    def block_of(axis_at):
        return (jnp.arange(drawn.shape[axis_at]) // (drawn.shape[axis_at] // shards_of)).reshape((-1,) + (1,) * (drawn.ndim - 1 - axis_at))

    first = jax.random.permutation(rng, shards_of)[block_of(target)]
    second = (block_of(target) + shards_of // 2) % shards_of
    return jnp.where((block_of(source) == first) | (block_of(source) == second), factor * drawn, drawn)


def block_levels(stream_key, extent, cuts, smallest, largest):
    loudness, own = 1.0, jax.random.fold_in(stream_key, 6)
    for axis_at, parts in cuts:
        draws = jnp.exp(jax.random.uniform(jax.random.fold_in(own, axis_at), (parts,), jnp.float32, smallest / len(cuts), largest / len(cuts)))
        loudness = loudness * jnp.repeat(draws, extent[axis_at] // parts).reshape([-1 if axis == axis_at else 1 for axis in range(len(extent))])
    return loudness


def bell_draw(stream_key, dims, width, most, shards=(), kind=jnp.bfloat16):
    result = width * jax.random.normal(stream_key, dims, jnp.float32)
    if shards:
        result = result * block_levels(stream_key, dims, shards, -0.22, 0.18)
    return jnp.clip(result, -most, most).astype(kind)


def heavy_noise(stream_key, dims, scale, bound, cuts, heavy, dtype=jnp.bfloat16):
    drawn = scale * jax.random.normal(stream_key, dims, jnp.float32)
    if cuts:
        drawn = drawn * block_levels(stream_key, dims, cuts, -0.22, 0.18)
    return jnp.clip(spiked(drawn, jax.random.fold_in(stream_key, 3), *heavy), -bound, bound).astype(dtype)


def setup_inputs(seed: int = 0) -> dict:
    streams_of = jax.random.split(jax.random.key(seed), 9)
    inputs = bell_draw(streams_of[0], (SEQLEN, D), 1.0, 6.0, ((0, 8),))
    x_weight = heavy_noise(streams_of[1], (D, HEADS * HEAD_DIM), D ** -0.5, 0.125, ((0, 8), (1, 4)), (1, 0, 8, 2.0))
    b_values = bell_draw(streams_of[2], (SEQLEN, GROUPS, STATE), STATE ** -0.5, 0.5, ((0, 8),))
    c_values = bell_draw(streams_of[3], (SEQLEN, GROUPS, STATE), SPAN ** -0.5, 0.375, ((0, 8),))
    gate_z = bell_draw(streams_of[4], (SEQLEN, HEADS * HEAD_DIM), 1.0, 6.0, ((0, 8), (1, 4)))
    log_decay = draw_log_decay(jax.random.fold_in(streams_of[8], 71), 0)
    skip_gain = jnp.clip(0.5 + 1.0 * jax.random.uniform(streams_of[6], (HEADS,), jnp.float32) ** block_levels(streams_of[6], (HEADS,), ((0, 4),), -0.2, 0.2), 0.5, 1.5)
    grad_out = bell_draw(streams_of[7], (SEQLEN, HEADS * HEAD_DIM), 1.0, 6.0, ((0, 8), (1, 4)))
    return {"inputs": inputs, "x_weight": x_weight, "b_values": b_values, "c_values": c_values, "gate_z": gate_z, "log_decay": log_decay, "skip_gain": skip_gain, "grad_out": grad_out}


EXACT_MODE = lax.Precision.HIGHEST


def expand_groups(values):
    return jnp.repeat(values, HEADS // GROUPS, axis=1)


def decayed_scores(c_block, b_block, prefix):
    scores = jnp.einsum('thn,shn->hts', c_block.astype(jnp.float32), b_block.astype(jnp.float32), precision=EXACT_MODE)
    later = prefix.T[:, :, None]
    earlier = prefix.T[:, None, :]
    positions = jnp.arange(prefix.shape[0])
    causal = (positions[:, None] >= positions[None, :])[None, :, :]
    spacing = jnp.where(causal, later - earlier, 0.0)
    factors = jnp.where(causal, jnp.exp(spacing), 0.0)
    return (scores * factors).astype(jnp.bfloat16)


def reference(inputs, x_weight, b_values, c_values, gate_z, log_decay, skip_gain, grad_out):
    block_count = SEQLEN // SPAN
    x_values = jnp.dot(inputs, x_weight, preferred_element_type=jnp.float32).astype(jnp.bfloat16)
    x_blocks = x_values.reshape(block_count, SPAN, HEADS, HEAD_DIM)
    b_blocks = expand_groups(b_values).reshape(block_count, SPAN, HEADS, STATE)
    c_blocks = expand_groups(c_values).reshape(block_count, SPAN, HEADS, STATE)
    decay_blocks = log_decay.reshape(block_count, SPAN, HEADS)
    gate = gate_z.astype(jnp.float32).reshape(SEQLEN, HEADS, HEAD_DIM)
    upstream = grad_out.astype(jnp.float32).reshape(SEQLEN, HEADS, HEAD_DIM)
    sigma = jax.nn.sigmoid(gate)
    y_grad = upstream * gate * sigma
    grad_blocks = y_grad.reshape(block_count, SPAN, HEADS, HEAD_DIM)
    low_blocks = grad_blocks.astype(jnp.bfloat16)
    gain = skip_gain[None, :, None]

    def forward(state, items):
        x_block, b_block, c_block, decay_block = items
        prefix = jnp.cumsum(decay_block, axis=0)
        weights = decayed_scores(c_block, b_block, prefix)
        local = jnp.einsum('hts,shp->thp', weights.astype(jnp.float32), x_block.astype(jnp.float32), precision=EXACT_MODE)
        carried = jnp.exp(prefix)[:, :, None] * jnp.einsum('thn,hpn->thp', c_block.astype(jnp.float32), state, precision=EXACT_MODE)
        tails = jnp.exp(prefix[-1][None, :] - prefix)
        fresh = jnp.einsum('shp,shn->hpn', x_block.astype(jnp.float32) * tails[:, :, None], b_block.astype(jnp.float32), precision=EXACT_MODE)
        state = jnp.exp(prefix[-1])[:, None, None] * state + fresh
        return state, local + carried + gain * x_block.astype(jnp.float32)

    zero_state = jnp.zeros((HEADS, HEAD_DIM, STATE), jnp.float32)
    final_state, outputs = lax.scan(forward, zero_state, (x_blocks, b_blocks, c_blocks, decay_blocks))
    outputs = outputs.reshape(SEQLEN, HEADS, HEAD_DIM)
    z_grad = (upstream * outputs * sigma * (1.0 + gate * (1.0 - sigma))).astype(jnp.bfloat16)
    z_grad = z_grad.reshape(SEQLEN, HEADS * HEAD_DIM)

    def backward(carry, items):
        b_block, c_block, decay_block, grad_block, low_block = items
        prefix = jnp.cumsum(decay_block, axis=0)
        weights = decayed_scores(c_block, b_block, prefix)
        local = jnp.einsum('hts,thp->shp', weights.astype(jnp.float32), low_block.astype(jnp.float32), precision=EXACT_MODE)
        tails = jnp.exp(prefix[-1][None, :] - prefix)
        carried = tails[:, :, None] * jnp.einsum('shn,hpn->shp', b_block.astype(jnp.float32), carry, precision=EXACT_MODE)
        fresh = jnp.einsum('thp,thn->hpn', grad_block * jnp.exp(prefix)[:, :, None], c_block.astype(jnp.float32), precision=EXACT_MODE)
        carry = jnp.exp(prefix[-1])[:, None, None] * carry + fresh
        return carry, local + carried + gain * grad_block

    final_grad, x_grads = lax.scan(backward, zero_state, (b_blocks, c_blocks, decay_blocks, grad_blocks, low_blocks), reverse=True)
    x_grad = x_grads.reshape(SEQLEN, HEADS * HEAD_DIM).astype(jnp.bfloat16)
    group_width = HEADS // N_HEAD * HEAD_DIM
    total_sum = jnp.zeros((SEQLEN, D), jnp.float32)
    for group in range(N_HEAD):
        grad_part = x_grad[:, group * group_width:(group + 1) * group_width]
        weight_part = x_weight[:, group * group_width:(group + 1) * group_width]
        partial_low = jnp.dot(grad_part, weight_part.T, preferred_element_type=jnp.float32).astype(jnp.bfloat16)
        partial_low = lax.optimization_barrier(partial_low)
        total_sum = total_sum + partial_low.astype(jnp.float32)
    input_grad = total_sum.astype(jnp.bfloat16)
    return input_grad, z_grad
```

```python
import jax
import jax.numpy as jnp
from jax import lax
from jax.sharding import PartitionSpec as P
from jax.experimental import pallas as pl
from jax.experimental.pallas import tpu as pltpu

HEADS = 128
HEAD_DIM = 64
STATE = 128
GROUPS = 8
SPAN = 256


EXACT_MODE = lax.Precision.HIGHEST


def prefix_2(array, axis, combine, identity):
    size, place = (lax.axis_size(axis), lax.axis_index(axis))
    everything = jax.tree.map(
        lambda part, kind: lax.all_gather(part.astype(kind), axis),
        array,
        (jnp.bfloat16, jnp.bfloat16),
    )
    start = jax.tree.map(
        lambda part, zero: jnp.broadcast_to(jnp.asarray(zero, part.dtype), part.shape),
        array,
        identity,
    )

    def prefix_hop(k, before):
        reached = k < place
        new = combine(
            before, jax.tree.map(lambda part, own: part[k].astype(own.dtype), everything, array)
        )
        return jax.tree.map(lambda a, b: jnp.where(reached, a, b), new, before)

    return lax.fori_loop(0, size, prefix_hop, start)


def entering(value, axis, join, neutral):
    count, mine = (lax.axis_size(axis), lax.axis_index(axis))
    pieces = jax.tree.map(lambda part: lax.all_gather(part, axis), value)
    pieces = jax.tree.map(lambda part: part[::-1], pieces)
    mine = count - 1 - mine
    so_far = jax.tree.map(
        lambda part, zero: jnp.full_like(part, 0) + jnp.asarray(zero, part.dtype), value, neutral
    )

    def entering_hop(position, so_far):
        longer = join(so_far, jax.tree.map(lambda part: part[position], pieces))
        return jax.tree.map(lambda new, old: jnp.where(position < mine, new, old), longer, so_far)

    return lax.fori_loop(0, count - 1, entering_hop, so_far)


def decayed_scores(c_block, b_block, prefix):
    scores = jnp.einsum("thn,shn->hts", c_block, b_block, preferred_element_type=jnp.float32)
    later = prefix.T[:, :, None]
    earlier = prefix.T[:, None, :]
    positions = jnp.arange(prefix.shape[0])
    causal = (positions[:, None] >= positions[None, :])[None, :, :]
    spacing = jnp.where(causal, later - earlier, 0.0)
    factors = jnp.where(causal, jnp.exp(spacing), 0.0)
    return (scores * factors).astype(jnp.bfloat16)


def compose(earlier, later):
    return (earlier[0] * later[0], later[0][:, None, None] * earlier[1] + later[1])


def body(inputs, x_weight, b_values, c_values, gate_z, log_decay, skip_gain, grad_out):
    token_count = inputs.shape[0]
    head_count = log_decay.shape[1]
    width_here = x_weight.shape[1]
    block_count = token_count // SPAN
    full_weight = lax.all_gather(x_weight, "seq", axis=0, tiled=True)
    x_sums = jnp.dot(inputs, full_weight, preferred_element_type=jnp.float32)
    x_values = x_sums.astype(jnp.bfloat16)
    first_head = lax.axis_index("head") * head_count
    owners = (first_head + jnp.arange(head_count)) // (HEADS // GROUPS)
    picker = (owners[:, None] == jnp.arange(GROUPS)[None, :]).astype(jnp.bfloat16)
    b_heads = jnp.einsum(
        "tgn,hg->thn", b_values, picker, preferred_element_type=jnp.float32
    ).astype(jnp.bfloat16)
    c_heads = jnp.einsum(
        "tgn,hg->thn", c_values, picker, preferred_element_type=jnp.float32
    ).astype(jnp.bfloat16)
    x_blocks = x_values.reshape(block_count, SPAN, head_count, HEAD_DIM)
    b_blocks = b_heads.reshape(block_count, SPAN, head_count, STATE)
    c_blocks = c_heads.reshape(block_count, SPAN, head_count, STATE)
    prefix = jnp.cumsum(log_decay.reshape(block_count, SPAN, head_count), axis=1)
    totals = prefix[:, -1, :]
    gate = gate_z.astype(jnp.float32).reshape(token_count, head_count, HEAD_DIM)
    upstream = grad_out.astype(jnp.float32).reshape(token_count, head_count, HEAD_DIM)
    sigma = jax.nn.sigmoid(gate)
    y_grad = upstream * gate * sigma
    grad_blocks = y_grad.reshape(block_count, SPAN, head_count, HEAD_DIM)
    low_blocks = grad_blocks.astype(jnp.bfloat16)
    tails = jnp.exp(totals[:, None, :] - prefix)
    fresh_states = jnp.einsum(
        "kshp,kshn->khpn",
        x_blocks.astype(jnp.float32) * tails[..., None],
        b_blocks.astype(jnp.float32),
        precision=EXACT_MODE,
    )
    fresh_grads = jnp.einsum(
        "kthp,kthn->khpn",
        grad_blocks * jnp.exp(prefix)[..., None],
        c_blocks.astype(jnp.float32),
        precision=EXACT_MODE,
    )
    running = jnp.cumsum(totals, axis=0)
    after = running[-1][None, :] - running
    before = running - totals
    device_decay = jnp.exp(running[-1])
    device_state = jnp.einsum("kh,khpn->hpn", jnp.exp(after), fresh_states, precision=EXACT_MODE)
    device_grad = jnp.einsum("kh,khpn->hpn", jnp.exp(before), fresh_grads, precision=EXACT_MODE)
    unit_decay = jnp.ones((head_count,), jnp.float32)
    start_state = prefix_2(
        (device_decay, device_state), "seq", compose, (unit_decay, jnp.zeros_like(device_state))
    )[1]
    end_grad = entering(
        (device_decay, device_grad), "seq", compose, (unit_decay, jnp.zeros_like(device_grad))
    )[1]
    gain = skip_gain[None, :, None]

    def forward(state, items):
        x_block, b_block, c_block, prefix_block, fresh = items
        weights = decayed_scores(c_block, b_block, prefix_block)
        local = jnp.einsum("hts,shp->thp", weights, x_block, preferred_element_type=jnp.float32)
        carried = jnp.exp(prefix_block)[:, :, None] * jnp.einsum(
            "thn,hpn->thp", c_block.astype(jnp.float32), state, precision=EXACT_MODE
        )
        state = jnp.exp(prefix_block[-1])[:, None, None] * state + fresh
        return (state, (local + carried + gain * x_block.astype(jnp.float32), weights))

    final_state, (outputs, weight_blocks) = lax.scan(
        forward, start_state, (x_blocks, b_blocks, c_blocks, prefix, fresh_states)
    )
    outputs = outputs.reshape(token_count, head_count, HEAD_DIM)
    z_grad = (upstream * outputs * sigma * (1.0 + gate * (1.0 - sigma))).astype(jnp.bfloat16)
    z_grad = z_grad.reshape(token_count, width_here)

    def backward(carry, items):
        weights, b_block, tail_block, total_block, grad_block, low_block, fresh = items
        local = jnp.einsum("hts,thp->shp", weights, low_block, preferred_element_type=jnp.float32)
        carried = tail_block[:, :, None] * jnp.einsum(
            "shn,hpn->shp", b_block.astype(jnp.float32), carry, precision=EXACT_MODE
        )
        carry = jnp.exp(total_block)[:, None, None] * carry + fresh
        return (carry, local + carried + gain * grad_block)

    final_grad, x_grads = lax.scan(
        backward,
        end_grad,
        (weight_blocks, b_blocks, tails, totals, grad_blocks, low_blocks, fresh_grads),
        reverse=True,
    )
    x_grad = x_grads.reshape(token_count, width_here).astype(jnp.bfloat16)
    partial_sums = jnp.einsum("tk,dk->td", x_grad, full_weight, preferred_element_type=jnp.float32)
    input_grad = lax.psum_scatter(
        partial_sums.astype(jnp.bfloat16), "head", scatter_dimension=1, tiled=True
    )
    return (input_grad, z_grad)


SEQ = 8
RUNS = 4
F32 = jnp.float32
BF16 = jnp.bfloat16


def dot_nn(a, b):
    return lax.dot_general(a, b, (((1,), (0,)), ((), ())), preferred_element_type=F32)


def dot_nt(a, b):
    return lax.dot_general(a, b, (((1,), (1,)), ((), ())), preferred_element_type=F32)


def dot_tn(a, b):
    return lax.dot_general(a, b, (((0,), (0,)), ((), ())), preferred_element_type=F32)


def mixer_kernel(
    inputs, w_hbm, b2, c2, gz, go, pexp, prow, gain, tt,
    out_ref, zg_ref,
    wbuf, xacc, xg, xg16, ysc, wts, gmat, x16, pbuf, rsbuf,
    fbuf, rf, sb, rr, rt,
    wsend, wrecv, wlocal, tsend, trecv, esend, erecv, rsend, rrecv,
):
    s = lax.axis_index("seq")
    z = lax.axis_index("head")
    core, xx, yy = s % 2, (s // 2) % 2, s // 4
    half = w_hbm.shape[1]
    heads = wts.shape[0]
    pairs = heads // 2
    per_group = pairs // b2.shape[0]

    def peer(r):
        a = (1 - core) if r & 1 else core
        b = (1 - xx) if r & 2 else xx
        c = (1 - yy) if r & 4 else yy
        return c * 4 + b * 2 + a

    def peer_dyn(r):
        a = (core + r) % 2
        b = (xx + r // 2) % 2
        c = (yy + r // 4) % 2
        return c * 4 + b * 2 + a

    barrier = pltpu.get_barrier_semaphore()
    for r in range(1, SEQ):
        pl.semaphore_signal(barrier, inc=1, device_id={"seq": peer(r)}, device_id_type=pl.DeviceIdType.MESH)
    for dz in range(1, RUNS):
        pl.semaphore_signal(barrier, inc=1, device_id={"head": (z + dz) % RUNS}, device_id_type=pl.DeviceIdType.MESH)
    pl.semaphore_wait(barrier, SEQ - 1 + RUNS - 1)

    def wcopy(src_slot, dst_slot, h, to):
        src = w_hbm.at[h] if src_slot == 0 else wbuf.at[src_slot, h]
        return pltpu.make_async_remote_copy(
            src_ref=src, dst_ref=wbuf.at[dst_slot, h],
            send_sem=wsend.at[dst_slot, h], recv_sem=wrecv.at[dst_slot, h],
            device_id={"seq": peer(to)}, device_id_type=pl.DeviceIdType.MESH)

    own = pltpu.make_async_copy(w_hbm, wbuf.at[0], wlocal)
    sent = []

    def go_send(src_slot, dst_slot, h, to):
        cp = wcopy(src_slot, dst_slot, h, to)
        cp.start()
        sent.append(cp)

    def w_wait(slot, h, to):
        wcopy(0, slot, h, to).wait_recv()

    def tcopy(r, slot):
        k = peer(r)
        return pltpu.make_async_remote_copy(
            src_ref=tt.at[k], dst_ref=rt.at[slot], send_sem=tsend.at[r], recv_sem=trecv.at[slot],
            device_id={"seq": k}, device_id_type=pl.DeviceIdType.MESH)

    for r in range(1, SEQ):
        tcopy(r, s).start()
    go_send(0, 2, 0, 2)
    go_send(0, 4, 1, 4)
    go_send(0, 2, 1, 2)
    go_send(0, 4, 0, 4)
    own.start()
    go_send(0, 1, 0, 1)
    go_send(0, 1, 1, 1)

    rt[s] = tt[s]
    for g in range(b2.shape[0]):
        gmat[g] = dot_nt(c2[g], b2[g])
    xacc[...] = jnp.zeros_like(xacc)
    lanes = lax.broadcasted_iota(jnp.int32, (SPAN, 128), 1)
    left = lanes < HEAD_DIM
    causal = lax.broadcasted_iota(jnp.int32, (SPAN, SPAN), 0) >= lax.broadcasted_iota(jnp.int32, (SPAN, SPAN), 1)

    def columns_of(i):
        return pl.ds(pl.multiple_of(i * 128, 128), 128)

    def back_pair(i, carry):
        cols = columns_of(i)
        gate = gz[:, cols].astype(F32)
        up = go[:, cols].astype(F32)
        grad = up * gate * jax.nn.sigmoid(gate)
        low = grad.astype(BF16)
        pe = pexp[i]
        ysc[:, cols] = (grad * jnp.exp(pe)).astype(BF16)
        scores = gmat[i // per_group]
        acc = []
        for k in range(2):
            later = pe[:, HEAD_DIM * k:HEAD_DIM * k + 1]
            earlier = prow[i, k:k + 1, :]
            factors = jnp.exp(jnp.where(causal, later - earlier, -1e30))
            w = (scores * factors).astype(BF16)
            wts[2 * i + k] = w
            acc.append(dot_tn(w, low))
        xg[:, cols] = jnp.where(left, acc[0], acc[1]) + gain[:, cols] * grad
        return carry

    lax.fori_loop(0, pairs, back_pair, 0)

    def ecopy(e, f, r, slot):
        k = peer(r)
        src, dst = (fbuf, rf) if f == 0 else (sb, rr)
        return pltpu.make_async_remote_copy(
            src_ref=src.at[e, k], dst_ref=dst.at[e, slot],
            send_sem=esend.at[e, f, r], recv_sem=erecv.at[e, f, slot],
            device_id={"seq": k}, device_id_type=pl.DeviceIdType.MESH)

    def e_start(e, f):
        for r in range(1, SEQ):
            ecopy(e, f, r, s).start()
        if f == 0:
            rf[e, s] = fbuf[e, s]
        else:
            rr[e, s] = sb[e, s]

    def e_wait(e, f):
        for r in range(1, SEQ):
            ecopy(e, f, r, peer(r)).wait_recv()

    def fresh(e, src, maps):
        def one(j, carry):
            cols = pl.ds(pl.multiple_of(j * 256, 256), 256)
            fbuf[e, j] = dot_tn(src[:, cols], maps[j // (SEQ // b2.shape[0])]).astype(BF16)
            return carry

        lax.fori_loop(0, SEQ, one, 0)

    def scan_states(e, order):
        per = heads // SEQ
        run = [jnp.zeros((HEAD_DIM, STATE), F32) for _ in range(per)]
        for k in order:
            decay = jnp.exp(rt[k])
            for m in range(per):
                rows = slice(m * HEAD_DIM, (m + 1) * HEAD_DIM)
                sb[e, k, rows, :] = run[m].astype(BF16)
                run[m] = run[m] * decay[m:m + 1, :] + rf[e, k, rows, :].astype(F32)

    def x_part(first, count):
        def one(i, carry):
            slot, h = i // 2, i % 2
            start = peer_dyn(slot) * 2 * half + h * half
            a = inputs[:, pl.ds(pl.multiple_of(start, 256), half)]
            for q in range(4):
                cs = slice(q * 512, (q + 1) * 512)
                xacc[:, cs] += dot_nn(a, wbuf[slot, h, :, cs])
            return carry

        lax.fori_loop(first, first + count, one, 0)

    def rcopy(i, src_z, target):
        slot, h = i // 2, i % 2
        piece = (peer_dyn(slot) % 2) * 2 + h
        return pltpu.make_async_remote_copy(
            src_ref=pbuf.at[i], dst_ref=rsbuf.at[src_z, piece],
            send_sem=rsend.at[i], recv_sem=rrecv.at[src_z, piece],
            device_id={"head": target}, device_id_type=pl.DeviceIdType.MESH)

    def p_part(first, count):
        def one(i, carry):
            slot, h = i // 2, i % 2
            owner = peer_dyn(slot)
            part = dot_nt(xg16[...], wbuf[slot, h]).astype(BF16)
            target = owner // 2

            @pl.when(target == z)
            def _():
                rsbuf[z, (owner % 2) * 2 + h] = part

            @pl.when(target != z)
            def _():
                pbuf[i] = part
                rcopy(i, z, target).start()

            return carry

        lax.fori_loop(first, first + count, one, 0)

    fresh(0, ysc, c2)
    e_start(0, 0)
    own.wait()
    x_part(0, 2)
    for r in range(1, SEQ):
        tcopy(r, peer(r)).wait_recv()
    e_wait(0, 0)
    scan_states(0, range(SEQ - 1, -1, -1))
    e_start(0, 1)
    w_wait(1, 0, 1)
    w_wait(1, 1, 1)
    x_part(2, 2)
    e_wait(0, 1)

    def back_finish(i, carry):
        cols = columns_of(i)
        state = rr[0, i // 2, pl.ds(pl.multiple_of((i % 2) * 128, 128), 128), :]
        pe = pexp[i]
        tail = jnp.exp(pe[SPAN - 1:SPAN, :] - pe)
        xg16[:, cols] = (xg[:, cols] + tail * dot_nt(b2[i // per_group], state)).astype(BF16)
        return carry

    lax.fori_loop(0, pairs, back_finish, 0)
    w_wait(2, 0, 2)
    go_send(2, 6, 0, 4)
    go_send(2, 3, 0, 1)
    w_wait(4, 1, 4)
    go_send(4, 6, 1, 2)
    go_send(4, 5, 1, 1)
    p_part(0, 4)
    w_wait(2, 1, 2)
    go_send(2, 3, 1, 1)
    w_wait(4, 0, 4)
    go_send(4, 5, 0, 1)
    x_part(4, 2)
    p_part(4, 2)
    x_part(8, 2)
    p_part(8, 2)
    for h in range(2):
        w_wait(3, h, 1)
        w_wait(5, h, 1)
    x_part(6, 2)
    p_part(6, 2)
    x_part(10, 2)
    p_part(10, 2)
    w_wait(6, 0, 4)
    go_send(6, 7, 0, 1)
    w_wait(6, 1, 2)
    go_send(6, 7, 1, 1)
    x_part(12, 2)
    w_wait(7, 0, 1)
    w_wait(7, 1, 1)
    x_part(14, 2)

    def fore_scale(i, carry):
        cols = columns_of(i)
        x = xacc[:, cols].astype(BF16)
        x16[:, cols] = x
        pe = pexp[i]
        ysc[:, cols] = (x.astype(F32) * jnp.exp(pe[SPAN - 1:SPAN, :] - pe)).astype(BF16)
        return carry

    lax.fori_loop(0, pairs, fore_scale, 0)
    fresh(1, ysc, b2)
    e_start(1, 0)
    p_part(12, 4)
    e_wait(1, 0)
    scan_states(1, range(SEQ))
    e_start(1, 1)

    def fore_local(i, carry):
        cols = columns_of(i)
        x = x16[:, cols]
        y = jnp.where(left, dot_nn(wts[2 * i], x), dot_nn(wts[2 * i + 1], x))
        xacc[:, cols] = y + gain[:, cols] * x.astype(F32)
        return carry

    lax.fori_loop(0, pairs, fore_local, 0)
    e_wait(1, 1)

    def fore_finish(i, carry):
        cols = columns_of(i)
        state = rr[1, i // 2, pl.ds(pl.multiple_of((i % 2) * 128, 128), 128), :]
        y = xacc[:, cols] + jnp.exp(pexp[i]) * dot_nt(c2[i // per_group], state)
        gate = gz[:, cols].astype(F32)
        up = go[:, cols].astype(F32)
        sigma = jax.nn.sigmoid(gate)
        zg_ref[:, cols] = (up * y * sigma * (1.0 + gate * (1.0 - sigma))).astype(BF16)
        return carry

    lax.fori_loop(0, pairs, fore_finish, 0)

    for dz in range(1, RUNS):
        source = (z + dz) % RUNS
        for piece in range(4):
            pltpu.make_async_remote_copy(
                src_ref=pbuf.at[0], dst_ref=rsbuf.at[source, piece],
                send_sem=rsend.at[0], recv_sem=rrecv.at[source, piece],
                device_id={"head": source}, device_id_type=pl.DeviceIdType.MESH).wait_recv()
    for piece in range(4):
        total = rsbuf[0, piece].astype(F32)
        for k in range(1, RUNS):
            total = total + rsbuf[k, piece].astype(F32)
        out_ref[:, piece * 256:(piece + 1) * 256] = total.astype(BF16)

    def drain(i, carry):
        @pl.when(peer_dyn(i // 2) // 2 != z)
        def _():
            rcopy(i, z, peer_dyn(i // 2) // 2).wait_send()

        return carry

    lax.fori_loop(0, 16, drain, 0)
    for cp in sent:
        cp.wait_send()
    for r in range(1, SEQ):
        tcopy(r, s).wait_send()
        for e in range(2):
            for f in range(2):
                ecopy(e, f, r, s).wait_send()


def fused_body(inputs, x_weight, b_values, c_values, gate_z, log_decay, skip_gain, grad_out):
    heads = log_decay.shape[1]
    width = x_weight.shape[1]
    depth = x_weight.shape[0]
    pairs = heads // 2
    groups = heads * GROUPS // HEADS
    z = lax.axis_index("head")
    b2 = jnp.swapaxes(lax.dynamic_slice_in_dim(b_values, z * groups, groups, 1), 0, 1)
    c2 = jnp.swapaxes(lax.dynamic_slice_in_dim(c_values, z * groups, groups, 1), 0, 1)
    prefix = jnp.cumsum(log_decay, axis=0)
    prow = prefix.T.reshape(pairs, 2, SPAN)
    pexp = jnp.broadcast_to(prow.swapaxes(1, 2)[..., None], (pairs, SPAN, 2, HEAD_DIM)).reshape(pairs, SPAN, 128)
    totals = prefix[-1].reshape(SEQ, 1, heads // SEQ)
    tt = jnp.broadcast_to(totals, (SEQ, 8 * SEQ // heads, heads // SEQ)).reshape(SEQ, 8, 1)
    tt = jnp.broadcast_to(tt, (SEQ, 8, 128))
    gain = jnp.repeat(skip_gain, HEAD_DIM)[None, :]
    halves = x_weight.reshape(2, depth // 2, width)
    vmem = pl.BlockSpec(memory_space=pltpu.VMEM)
    tokens = inputs.shape[0]
    dma = pltpu.SemaphoreType.DMA
    state = (2, SEQ, heads // SEQ * HEAD_DIM, STATE)
    return tuple(pl.pallas_call(
        mixer_kernel,
        out_shape=(
            jax.ShapeDtypeStruct((tokens, inputs.shape[1] // RUNS), BF16),
            jax.ShapeDtypeStruct((tokens, width), BF16),
        ),
        in_specs=[vmem, pl.BlockSpec(memory_space=pl.ANY)] + [vmem] * 8,
        out_specs=(vmem, vmem),
        scratch_shapes=[
            pltpu.VMEM((SEQ, 2, depth // 2, width), BF16),
            pltpu.VMEM((tokens, width), F32),
            pltpu.VMEM((tokens, width), F32),
            pltpu.VMEM((tokens, width), BF16),
            pltpu.VMEM((tokens, width), BF16),
            pltpu.VMEM((heads, SPAN, SPAN), BF16),
            pltpu.VMEM((groups, SPAN, SPAN), F32),
            pltpu.VMEM((tokens, width), BF16),
            pltpu.VMEM((2 * SEQ, tokens, depth // 2), BF16),
            pltpu.VMEM((RUNS, 4, tokens, depth // 2), BF16),
            pltpu.VMEM(state, BF16),
            pltpu.VMEM(state, BF16),
            pltpu.VMEM(state, BF16),
            pltpu.VMEM(state, BF16),
            pltpu.VMEM((SEQ, 8, 128), F32),
            dma((SEQ, 2)), dma((SEQ, 2)), dma,
            dma((SEQ,)), dma((SEQ,)),
            dma((2, 2, SEQ)), dma((2, 2, SEQ)),
            dma((2 * SEQ,)), dma((RUNS, 4)),
        ],
        compiler_params=pltpu.CompilerParams(
            collective_id=0, has_side_effects=True, vmem_limit_bytes=60 * 1024 * 1024),
        name="mixer",
    )(inputs, halves, b2, c2, gate_z, grad_out, pexp, prow, gain, tt))


def solution(mesh):
    in_specs = (
        P("seq", None),
        P("seq", "head"),
        P("seq", None, None),
        P("seq", None, None),
        P("seq", "head"),
        P("seq", "head"),
        P("head"),
        P("seq", "head"),
    )
    out_specs = (P("seq", "head"), P("seq", "head"))
    small = mesh.shape["seq"] == SEQ and mesh.shape["head"] == RUNS
    chosen = fused_body if small else body
    return jax.shard_map(chosen, mesh=mesh, in_specs=in_specs, out_specs=out_specs, check_vma=False)
```

```python
import jax
import jax.numpy as jnp
from jax import lax
from jax.sharding import PartitionSpec as P
from jax.experimental import pallas as pl
from jax.experimental.pallas import tpu as pltpu

HEADS = 128
HEAD_DIM = 64
STATE = 128
GROUPS = 8
SPAN = 256


EXACT_MODE = lax.Precision.HIGHEST


def prefix_2(array, axis, combine, identity):
    size, place = (lax.axis_size(axis), lax.axis_index(axis))
    everything = jax.tree.map(
        lambda part, kind: lax.all_gather(part.astype(kind), axis),
        array,
        (jnp.bfloat16, jnp.bfloat16),
    )
    start = jax.tree.map(
        lambda part, zero: jnp.broadcast_to(jnp.asarray(zero, part.dtype), part.shape),
        array,
        identity,
    )

    def prefix_hop(k, before):
        reached = k < place
        new = combine(
            before, jax.tree.map(lambda part, own: part[k].astype(own.dtype), everything, array)
        )
        return jax.tree.map(lambda a, b: jnp.where(reached, a, b), new, before)

    return lax.fori_loop(0, size, prefix_hop, start)


def entering(value, axis, join, neutral):
    count, mine = (lax.axis_size(axis), lax.axis_index(axis))
    pieces = jax.tree.map(lambda part: lax.all_gather(part, axis), value)
    pieces = jax.tree.map(lambda part: part[::-1], pieces)
    mine = count - 1 - mine
    so_far = jax.tree.map(
        lambda part, zero: jnp.full_like(part, 0) + jnp.asarray(zero, part.dtype), value, neutral
    )

    def entering_hop(position, so_far):
        longer = join(so_far, jax.tree.map(lambda part: part[position], pieces))
        return jax.tree.map(lambda new, old: jnp.where(position < mine, new, old), longer, so_far)

    return lax.fori_loop(0, count - 1, entering_hop, so_far)


def decayed_scores(c_block, b_block, prefix):
    scores = jnp.einsum("thn,shn->hts", c_block, b_block, preferred_element_type=jnp.float32)
    later = prefix.T[:, :, None]
    earlier = prefix.T[:, None, :]
    positions = jnp.arange(prefix.shape[0])
    causal = (positions[:, None] >= positions[None, :])[None, :, :]
    spacing = jnp.where(causal, later - earlier, 0.0)
    factors = jnp.where(causal, jnp.exp(spacing), 0.0)
    return (scores * factors).astype(jnp.bfloat16)


def compose(earlier, later):
    return (earlier[0] * later[0], later[0][:, None, None] * earlier[1] + later[1])


def body(inputs, x_weight, b_values, c_values, gate_z, log_decay, skip_gain, grad_out):
    token_count = inputs.shape[0]
    head_count = log_decay.shape[1]
    width_here = x_weight.shape[1]
    block_count = token_count // SPAN
    full_weight = lax.all_gather(x_weight, "seq", axis=0, tiled=True)
    x_sums = jnp.dot(inputs, full_weight, preferred_element_type=jnp.float32)
    x_values = x_sums.astype(jnp.bfloat16)
    first_head = lax.axis_index("head") * head_count
    owners = (first_head + jnp.arange(head_count)) // (HEADS // GROUPS)
    picker = (owners[:, None] == jnp.arange(GROUPS)[None, :]).astype(jnp.bfloat16)
    b_heads = jnp.einsum(
        "tgn,hg->thn", b_values, picker, preferred_element_type=jnp.float32
    ).astype(jnp.bfloat16)
    c_heads = jnp.einsum(
        "tgn,hg->thn", c_values, picker, preferred_element_type=jnp.float32
    ).astype(jnp.bfloat16)
    x_blocks = x_values.reshape(block_count, SPAN, head_count, HEAD_DIM)
    b_blocks = b_heads.reshape(block_count, SPAN, head_count, STATE)
    c_blocks = c_heads.reshape(block_count, SPAN, head_count, STATE)
    prefix = jnp.cumsum(log_decay.reshape(block_count, SPAN, head_count), axis=1)
    totals = prefix[:, -1, :]
    gate = gate_z.astype(jnp.float32).reshape(token_count, head_count, HEAD_DIM)
    upstream = grad_out.astype(jnp.float32).reshape(token_count, head_count, HEAD_DIM)
    sigma = jax.nn.sigmoid(gate)
    y_grad = upstream * gate * sigma
    grad_blocks = y_grad.reshape(block_count, SPAN, head_count, HEAD_DIM)
    low_blocks = grad_blocks.astype(jnp.bfloat16)
    tails = jnp.exp(totals[:, None, :] - prefix)
    fresh_states = jnp.einsum(
        "kshp,kshn->khpn",
        x_blocks.astype(jnp.float32) * tails[..., None],
        b_blocks.astype(jnp.float32),
        precision=EXACT_MODE,
    )
    fresh_grads = jnp.einsum(
        "kthp,kthn->khpn",
        grad_blocks * jnp.exp(prefix)[..., None],
        c_blocks.astype(jnp.float32),
        precision=EXACT_MODE,
    )
    running = jnp.cumsum(totals, axis=0)
    after = running[-1][None, :] - running
    before = running - totals
    device_decay = jnp.exp(running[-1])
    device_state = jnp.einsum("kh,khpn->hpn", jnp.exp(after), fresh_states, precision=EXACT_MODE)
    device_grad = jnp.einsum("kh,khpn->hpn", jnp.exp(before), fresh_grads, precision=EXACT_MODE)
    unit_decay = jnp.ones((head_count,), jnp.float32)
    start_state = prefix_2(
        (device_decay, device_state), "seq", compose, (unit_decay, jnp.zeros_like(device_state))
    )[1]
    end_grad = entering(
        (device_decay, device_grad), "seq", compose, (unit_decay, jnp.zeros_like(device_grad))
    )[1]
    gain = skip_gain[None, :, None]

    def forward(state, items):
        x_block, b_block, c_block, prefix_block, fresh = items
        weights = decayed_scores(c_block, b_block, prefix_block)
        local = jnp.einsum("hts,shp->thp", weights, x_block, preferred_element_type=jnp.float32)
        carried = jnp.exp(prefix_block)[:, :, None] * jnp.einsum(
            "thn,hpn->thp", c_block.astype(jnp.float32), state, precision=EXACT_MODE
        )
        state = jnp.exp(prefix_block[-1])[:, None, None] * state + fresh
        return (state, (local + carried + gain * x_block.astype(jnp.float32), weights))

    final_state, (outputs, weight_blocks) = lax.scan(
        forward, start_state, (x_blocks, b_blocks, c_blocks, prefix, fresh_states)
    )
    outputs = outputs.reshape(token_count, head_count, HEAD_DIM)
    z_grad = (upstream * outputs * sigma * (1.0 + gate * (1.0 - sigma))).astype(jnp.bfloat16)
    z_grad = z_grad.reshape(token_count, width_here)

    def backward(carry, items):
        weights, b_block, tail_block, total_block, grad_block, low_block, fresh = items
        local = jnp.einsum("hts,thp->shp", weights, low_block, preferred_element_type=jnp.float32)
        carried = tail_block[:, :, None] * jnp.einsum(
            "shn,hpn->shp", b_block.astype(jnp.float32), carry, precision=EXACT_MODE
        )
        carry = jnp.exp(total_block)[:, None, None] * carry + fresh
        return (carry, local + carried + gain * grad_block)

    final_grad, x_grads = lax.scan(
        backward,
        end_grad,
        (weight_blocks, b_blocks, tails, totals, grad_blocks, low_blocks, fresh_grads),
        reverse=True,
    )
    x_grad = x_grads.reshape(token_count, width_here).astype(jnp.bfloat16)
    partial_sums = jnp.einsum("tk,dk->td", x_grad, full_weight, preferred_element_type=jnp.float32)
    input_grad = lax.psum_scatter(
        partial_sums.astype(jnp.bfloat16), "head", scatter_dimension=1, tiled=True
    )
    return (input_grad, z_grad)


SEQ = 8
RUNS = 4
F32 = jnp.float32
BF16 = jnp.bfloat16


def dot_nn(a, b):
    return lax.dot_general(a, b, (((1,), (0,)), ((), ())), preferred_element_type=F32)


def dot_nt(a, b):
    return lax.dot_general(a, b, (((1,), (1,)), ((), ())), preferred_element_type=F32)


def dot_tn(a, b):
    return lax.dot_general(a, b, (((0,), (0,)), ((), ())), preferred_element_type=F32)


def mixer_kernel(
    in_hbm, w_hbm, b_flat, c_flat, gz_hbm, go_hbm, decay_ref, skip_ref,
    out_ref, zg_ref,
    inputs, gz, go, b2, c2, pexp, prow, gain, tt,
    wbuf, xacc, xg, xg16, ysc, wts, gmat, x16, pbuf, rin,
    fbuf, rf, sb, rr, rt,
    loads, wsend, wrecv, wlocal, tsend, trecv, esend, erecv, rsend, rrecv,
):
    s = lax.axis_index("seq")
    z = lax.axis_index("head")
    core, xx, yy = s % 2, (s // 2) % 2, s // 4
    half = w_hbm.shape[1]
    heads = wts.shape[0]
    pairs = heads // 2
    per_group = pairs // b2.shape[0]

    def peer(r):
        a = (1 - core) if r & 1 else core
        b = (1 - xx) if r & 2 else xx
        c = (1 - yy) if r & 4 else yy
        return c * 4 + b * 2 + a

    def peer_dyn(r):
        a = (core + r) % 2
        b = (xx + r // 2) % 2
        c = (yy + r // 4) % 2
        return c * 4 + b * 2 + a

    staged = [pltpu.make_async_copy(src, dst, loads.at[n]) for n, (src, dst) in enumerate(
        ((gz_hbm, gz), (go_hbm, go), (in_hbm, inputs)))]
    for cp in staged:
        cp.start()
    barrier = pltpu.get_barrier_semaphore()
    for r in range(1, SEQ):
        pl.semaphore_signal(barrier, inc=1, device_id={"seq": peer(r)}, device_id_type=pl.DeviceIdType.MESH)
    for dz in range(1, RUNS):
        pl.semaphore_signal(barrier, inc=1, device_id={"head": (z + dz) % RUNS}, device_id_type=pl.DeviceIdType.MESH)
    pl.semaphore_wait(barrier, SEQ - 1 + RUNS - 1)

    def wcopy(src_slot, dst_slot, h, to):
        src = w_hbm.at[h] if src_slot == 0 else wbuf.at[src_slot, h]
        return pltpu.make_async_remote_copy(
            src_ref=src, dst_ref=wbuf.at[dst_slot, h],
            send_sem=wsend.at[dst_slot, h], recv_sem=wrecv.at[dst_slot, h],
            device_id={"seq": peer(to)}, device_id_type=pl.DeviceIdType.MESH)

    own = pltpu.make_async_copy(w_hbm, wbuf.at[0], wlocal)
    sent = []

    def go_send(src_slot, dst_slot, h, to):
        cp = wcopy(src_slot, dst_slot, h, to)
        cp.start()
        sent.append(cp)

    def w_wait(slot, h, to):
        wcopy(0, slot, h, to).wait_recv()

    def tcopy(r, slot):
        k = peer(r)
        return pltpu.make_async_remote_copy(
            src_ref=tt.at[k], dst_ref=rt.at[slot], send_sem=tsend.at[r], recv_sem=trecv.at[slot],
            device_id={"seq": k}, device_id_type=pl.DeviceIdType.MESH)

    go_send(0, 2, 0, 2)
    go_send(0, 4, 1, 4)
    go_send(0, 2, 1, 2)
    go_send(0, 4, 0, 4)
    own.start()
    go_send(0, 1, 0, 1)
    go_send(0, 1, 1, 1)

    groups = b2.shape[0]
    for g in range(groups):
        span = pl.ds(pl.multiple_of((z * groups + g) * STATE, STATE), STATE)
        b2[g] = b_flat[:, span]
        c2[g] = c_flat[:, span]
    lower = (lax.broadcasted_iota(jnp.int32, (SPAN, SPAN), 0) >= lax.broadcasted_iota(jnp.int32, (SPAN, SPAN), 1))
    ones = jnp.where(lower, 1.0, 0.0).astype(F32)
    prefix = lax.dot_general(ones, decay_ref[...], (((1,), (0,)), ((), ())), preferred_element_type=F32, precision=EXACT_MODE)
    across = lax.dot_general(decay_ref[...], ones, (((0,), (1,)), ((), ())), preferred_element_type=F32, precision=EXACT_MODE)
    per_chunk = heads // SEQ
    closing = jnp.broadcast_to(across[:, SPAN - 1:SPAN], (heads, 128))
    tt[...] = jnp.zeros_like(tt)
    for j in range(SEQ):
        tt[j, 0:per_chunk, :] = closing[j * per_chunk:(j + 1) * per_chunk, :]
    for i in range(pairs):
        prow[i, 0:2, :] = across[2 * i:2 * i + 2, :]
    both = jnp.concatenate([prefix, jnp.broadcast_to(skip_ref[...], (8, heads))], axis=0)

    def expand_pair(i, carry):
        head = lax.broadcasted_iota(jnp.int32, (heads, 128), 0)
        lane = lax.broadcasted_iota(jnp.int32, (heads, 128), 1)
        pick = jnp.where(head == 2 * i + lane // HEAD_DIM, 1.0, 0.0).astype(F32)
        wide = lax.dot_general(both, pick, (((1,), (0,)), ((), ())), preferred_element_type=F32, precision=EXACT_MODE)
        pexp[i] = wide[:SPAN]
        gain[i] = wide[SPAN:]
        return carry

    lax.fori_loop(0, pairs, expand_pair, 0)
    rt[s] = tt[s]
    for r in range(1, SEQ):
        tcopy(r, s).start()
    staged[0].wait()
    staged[1].wait()
    for g in range(groups):
        gmat[g] = dot_nt(c2[g], b2[g])
    xacc[...] = jnp.zeros_like(xacc)
    lanes = lax.broadcasted_iota(jnp.int32, (SPAN, 128), 1)
    left = lanes < HEAD_DIM
    causal = lax.broadcasted_iota(jnp.int32, (SPAN, SPAN), 0) >= lax.broadcasted_iota(jnp.int32, (SPAN, SPAN), 1)

    def columns_of(i):
        return pl.ds(pl.multiple_of(i * 128, 128), 128)

    def back_pair(i, carry):
        cols = columns_of(i)
        gate = gz[:, cols].astype(F32)
        up = go[:, cols].astype(F32)
        grad = up * gate * jax.nn.sigmoid(gate)
        low = grad.astype(BF16)
        pe = pexp[i]
        ysc[:, cols] = (grad * jnp.exp(pe)).astype(BF16)
        scores = gmat[i // per_group]
        acc = []
        for k in range(2):
            later = pe[:, HEAD_DIM * k:HEAD_DIM * k + 1]
            earlier = prow[i, k:k + 1, :]
            factors = jnp.exp(jnp.where(causal, later - earlier, -1e30))
            w = (scores * factors).astype(BF16)
            wts[2 * i + k] = w
            acc.append(dot_tn(w, low))
        xg[:, cols] = jnp.where(left, acc[0], acc[1]) + gain[i, 0:1, :] * grad
        return carry

    lax.fori_loop(0, pairs, back_pair, 0)

    def ecopy(e, f, r, slot):
        k = peer(r)
        src, dst = (fbuf, rf) if f == 0 else (sb, rr)
        return pltpu.make_async_remote_copy(
            src_ref=src.at[e, k], dst_ref=dst.at[e, slot],
            send_sem=esend.at[e, f, r], recv_sem=erecv.at[e, f, slot],
            device_id={"seq": k}, device_id_type=pl.DeviceIdType.MESH)

    def e_start(e, f):
        for r in range(1, SEQ):
            ecopy(e, f, r, s).start()
        if f == 0:
            rf[e, s] = fbuf[e, s]
        else:
            rr[e, s] = sb[e, s]

    def e_wait(e, f):
        for r in range(1, SEQ):
            ecopy(e, f, r, peer(r)).wait_recv()

    def fresh(e, src, maps):
        def one(j, carry):
            cols = pl.ds(pl.multiple_of(j * 256, 256), 256)
            fbuf[e, j] = dot_tn(src[:, cols], maps[j // (SEQ // b2.shape[0])]).astype(BF16)
            return carry

        lax.fori_loop(0, SEQ, one, 0)

    def scan_states(e, order):
        per = heads // SEQ
        run = [jnp.zeros((HEAD_DIM, STATE), F32) for _ in range(per)]
        for k in order:
            decay = jnp.exp(rt[k])
            for m in range(per):
                rows = slice(m * HEAD_DIM, (m + 1) * HEAD_DIM)
                sb[e, k, rows, :] = run[m].astype(BF16)
                run[m] = run[m] * decay[m:m + 1, :] + rf[e, k, rows, :].astype(F32)

    def x_part(first, count):
        def one(i, carry):
            slot, h = i // 2, i % 2
            start = peer_dyn(slot) * 2 * half + h * half
            a = inputs[:, pl.ds(pl.multiple_of(start, 256), half)]
            for q in range(4):
                cs = slice(q * 512, (q + 1) * 512)
                xacc[:, cs] += dot_nn(a, wbuf[slot, h, :, cs])
            return carry

        lax.fori_loop(first, first + count, one, 0)

    def route(i):
        target = peer_dyn(i // 2) // 2
        up = (z + RUNS - 1 - target) // RUNS
        return target, up, up * (RUNS - 1)

    def rcopy(i, up):
        return pltpu.make_async_remote_copy(
            src_ref=pbuf.at[i], dst_ref=rin.at[up, i],
            send_sem=rsend.at[i], recv_sem=rrecv.at[up, i],
            device_id={"head": (z + 1 + up * 2) % RUNS}, device_id_type=pl.DeviceIdType.MESH)

    def p_part(first, count):
        def one(i, carry):
            slot, h = i // 2, i % 2
            target, up, edge = route(i)
            pbuf[i] = dot_nt(xg16[...], wbuf[slot, h]).astype(BF16)

            @pl.when((target != z) & (z == edge))
            def _():
                rcopy(i, up).start()

            return carry

        lax.fori_loop(first, first + count, one, 0)

    def p_pass(first, count):
        def one(i, carry):
            target, up, edge = route(i)

            @pl.when((target != z) & (z != edge))
            def _():
                rcopy(i, up).wait_recv()
                pbuf[i] = (pbuf[i].astype(F32) + rin[up, i].astype(F32)).astype(BF16)
                rcopy(i, up).start()

            return carry

        lax.fori_loop(first, first + count, one, 0)

    fresh(0, ysc, c2)
    e_start(0, 0)
    own.wait()
    staged[2].wait()
    x_part(0, 2)
    for r in range(1, SEQ):
        tcopy(r, peer(r)).wait_recv()
    e_wait(0, 0)
    scan_states(0, range(SEQ - 1, -1, -1))
    e_start(0, 1)
    w_wait(1, 0, 1)
    w_wait(1, 1, 1)
    x_part(2, 2)
    e_wait(0, 1)

    def back_finish(i, carry):
        cols = columns_of(i)
        state = rr[0, i // 2, pl.ds(pl.multiple_of((i % 2) * 128, 128), 128), :]
        pe = pexp[i]
        tail = jnp.exp(pe[SPAN - 1:SPAN, :] - pe)
        xg16[:, cols] = (xg[:, cols] + tail * dot_nt(b2[i // per_group], state)).astype(BF16)
        return carry

    lax.fori_loop(0, pairs, back_finish, 0)
    w_wait(2, 0, 2)
    go_send(2, 6, 0, 4)
    go_send(2, 3, 0, 1)
    w_wait(4, 1, 4)
    go_send(4, 6, 1, 2)
    go_send(4, 5, 1, 1)
    p_part(0, 4)
    w_wait(2, 1, 2)
    go_send(2, 3, 1, 1)
    w_wait(4, 0, 4)
    go_send(4, 5, 0, 1)
    x_part(4, 2)
    p_part(4, 2)
    x_part(8, 2)
    p_part(8, 2)
    p_pass(0, 4)
    for h in range(2):
        w_wait(3, h, 1)
        w_wait(5, h, 1)
    x_part(6, 2)
    p_part(6, 2)
    x_part(10, 2)
    p_part(10, 2)
    w_wait(6, 0, 4)
    go_send(6, 7, 0, 1)
    w_wait(6, 1, 2)
    go_send(6, 7, 1, 1)
    x_part(12, 2)
    p_pass(4, 8)
    w_wait(7, 0, 1)
    w_wait(7, 1, 1)
    x_part(14, 2)

    def fore_scale(i, carry):
        cols = columns_of(i)
        x = xacc[:, cols].astype(BF16)
        x16[:, cols] = x
        pe = pexp[i]
        ysc[:, cols] = (x.astype(F32) * jnp.exp(pe[SPAN - 1:SPAN, :] - pe)).astype(BF16)
        return carry

    lax.fori_loop(0, pairs, fore_scale, 0)
    fresh(1, ysc, b2)
    e_start(1, 0)
    p_part(12, 4)
    e_wait(1, 0)
    scan_states(1, range(SEQ))
    e_start(1, 1)
    p_pass(12, 4)

    def fore_local(i, carry):
        cols = columns_of(i)
        x = x16[:, cols]
        y = jnp.where(left, dot_nn(wts[2 * i], x), dot_nn(wts[2 * i + 1], x))
        xacc[:, cols] = y + gain[i, 0:1, :] * x.astype(F32)
        return carry

    lax.fori_loop(0, pairs, fore_local, 0)
    e_wait(1, 1)

    def fore_finish(i, carry):
        cols = columns_of(i)
        state = rr[1, i // 2, pl.ds(pl.multiple_of((i % 2) * 128, 128), 128), :]
        y = xacc[:, cols] + jnp.exp(pexp[i]) * dot_nt(c2[i // per_group], state)
        gate = gz[:, cols].astype(F32)
        up = go[:, cols].astype(F32)
        sigma = jax.nn.sigmoid(gate)
        zg_ref[:, cols] = (up * y * sigma * (1.0 + gate * (1.0 - sigma))).astype(BF16)
        return carry

    lax.fori_loop(0, pairs, fore_finish, 0)

    def gather_own(i, carry):
        owner = peer_dyn(i // 2)

        @pl.when(owner // 2 == z)
        def _():
            piece = (owner % 2) * 2 + i % 2
            out_cols = pl.ds(pl.multiple_of(piece * 256, 256), 256)
            xg[:, out_cols] = pbuf[i].astype(F32)

            @pl.when(z != 0)
            def _():
                rcopy(i, 0).wait_recv()
                xg[:, out_cols] += rin[0, i].astype(F32)

            @pl.when(z != RUNS - 1)
            def _():
                rcopy(i, 1).wait_recv()
                xg[:, out_cols] += rin[1, i].astype(F32)

            out_ref[:, out_cols] = xg[:, out_cols].astype(BF16)

        return carry

    lax.fori_loop(0, 16, gather_own, 0)

    def drain(i, carry):
        target, up, edge = route(i)

        @pl.when(target != z)
        def _():
            rcopy(i, up).wait_send()

        return carry

    lax.fori_loop(0, 16, drain, 0)
    for cp in sent:
        cp.wait_send()
    for r in range(1, SEQ):
        tcopy(r, s).wait_send()
        for e in range(2):
            for f in range(2):
                ecopy(e, f, r, s).wait_send()


def fused_body(inputs, x_weight, b_values, c_values, gate_z, log_decay, skip_gain, grad_out):
    heads = log_decay.shape[1]
    width = x_weight.shape[1]
    depth = x_weight.shape[0]
    pairs = heads // 2
    groups = heads * GROUPS // HEADS
    b_flat = b_values.reshape(b_values.shape[0], GROUPS * STATE)
    c_flat = c_values.reshape(c_values.shape[0], GROUPS * STATE)
    halves = x_weight.reshape(2, depth // 2, width)
    vmem = pl.BlockSpec(memory_space=pltpu.VMEM)
    hbm = pl.BlockSpec(memory_space=pl.ANY)
    tokens = inputs.shape[0]
    dma = pltpu.SemaphoreType.DMA
    state = (2, SEQ, heads // SEQ * HEAD_DIM, STATE)
    return tuple(pl.pallas_call(
        mixer_kernel,
        out_shape=(
            jax.ShapeDtypeStruct((tokens, inputs.shape[1] // RUNS), BF16),
            jax.ShapeDtypeStruct((tokens, width), BF16),
        ),
        in_specs=[hbm, hbm, vmem, vmem, hbm, hbm, vmem, vmem],
        out_specs=(vmem, vmem),
        scratch_shapes=[
            pltpu.VMEM(inputs.shape, BF16),
            pltpu.VMEM((tokens, width), BF16),
            pltpu.VMEM((tokens, width), BF16),
            pltpu.VMEM((groups, SPAN, STATE), BF16),
            pltpu.VMEM((groups, SPAN, STATE), BF16),
            pltpu.VMEM((pairs, SPAN, 128), F32),
            pltpu.VMEM((pairs, 8, SPAN), F32),
            pltpu.VMEM((pairs, 8, 128), F32),
            pltpu.VMEM((SEQ, 8, 128), F32),
            pltpu.VMEM((SEQ, 2, depth // 2, width), BF16),
            pltpu.VMEM((tokens, width), F32),
            pltpu.VMEM((tokens, width), F32),
            pltpu.VMEM((tokens, width), BF16),
            pltpu.VMEM((tokens, width), BF16),
            pltpu.VMEM((heads, SPAN, SPAN), BF16),
            pltpu.VMEM((groups, SPAN, SPAN), F32),
            pltpu.VMEM((tokens, width), BF16),
            pltpu.VMEM((2 * SEQ, tokens, depth // 2), BF16),
            pltpu.VMEM((2, 2 * SEQ, tokens, depth // 2), BF16),
            pltpu.VMEM(state, BF16),
            pltpu.VMEM(state, BF16),
            pltpu.VMEM(state, BF16),
            pltpu.VMEM(state, BF16),
            pltpu.VMEM((SEQ, 8, 128), F32),
            dma((3,)), dma((SEQ, 2)), dma((SEQ, 2)), dma,
            dma((SEQ,)), dma((SEQ,)),
            dma((2, 2, SEQ)), dma((2, 2, SEQ)),
            dma((2 * SEQ,)), dma((2, 2 * SEQ)),
        ],
        compiler_params=pltpu.CompilerParams(
            collective_id=0, has_side_effects=True, vmem_limit_bytes=60 * 1024 * 1024),
        name="mixer",
    )(inputs, halves, b_flat, c_flat, gate_z, grad_out, log_decay, skip_gain[None, :]))


def solution(mesh):
    in_specs = (
        P("seq", None),
        P("seq", "head"),
        P("seq", None, None),
        P("seq", None, None),
        P("seq", "head"),
        P("seq", "head"),
        P("head"),
        P("seq", "head"),
    )
    out_specs = (P("seq", "head"), P("seq", "head"))
    small = mesh.shape["seq"] == SEQ and mesh.shape["head"] == RUNS
    chosen = fused_body if small else body
    return jax.shard_map(chosen, mesh=mesh, in_specs=in_specs, out_specs=out_specs, check_vma=False)
```

```python
import jax
import jax.numpy as jnp
from jax import lax
from jax.sharding import PartitionSpec as P
from jax.experimental import pallas as pl
from jax.experimental.pallas import tpu as pltpu

HEADS = 128
HEAD_DIM = 64
STATE = 128
GROUPS = 8
SPAN = 256


EXACT_MODE = lax.Precision.HIGHEST


def prefix_2(array, axis, combine, identity):
    size, place = (lax.axis_size(axis), lax.axis_index(axis))
    everything = jax.tree.map(
        lambda part, kind: lax.all_gather(part.astype(kind), axis),
        array,
        (jnp.bfloat16, jnp.bfloat16),
    )
    start = jax.tree.map(
        lambda part, zero: jnp.broadcast_to(jnp.asarray(zero, part.dtype), part.shape),
        array,
        identity,
    )

    def prefix_hop(k, before):
        reached = k < place
        new = combine(
            before, jax.tree.map(lambda part, own: part[k].astype(own.dtype), everything, array)
        )
        return jax.tree.map(lambda a, b: jnp.where(reached, a, b), new, before)

    return lax.fori_loop(0, size, prefix_hop, start)


def entering(value, axis, join, neutral):
    count, mine = (lax.axis_size(axis), lax.axis_index(axis))
    pieces = jax.tree.map(lambda part: lax.all_gather(part, axis), value)
    pieces = jax.tree.map(lambda part: part[::-1], pieces)
    mine = count - 1 - mine
    so_far = jax.tree.map(
        lambda part, zero: jnp.full_like(part, 0) + jnp.asarray(zero, part.dtype), value, neutral
    )

    def entering_hop(position, so_far):
        longer = join(so_far, jax.tree.map(lambda part: part[position], pieces))
        return jax.tree.map(lambda new, old: jnp.where(position < mine, new, old), longer, so_far)

    return lax.fori_loop(0, count - 1, entering_hop, so_far)


def decayed_scores(c_block, b_block, prefix):
    scores = jnp.einsum("thn,shn->hts", c_block, b_block, preferred_element_type=jnp.float32)
    later = prefix.T[:, :, None]
    earlier = prefix.T[:, None, :]
    positions = jnp.arange(prefix.shape[0])
    causal = (positions[:, None] >= positions[None, :])[None, :, :]
    spacing = jnp.where(causal, later - earlier, 0.0)
    factors = jnp.where(causal, jnp.exp(spacing), 0.0)
    return (scores * factors).astype(jnp.bfloat16)


def compose(earlier, later):
    return (earlier[0] * later[0], later[0][:, None, None] * earlier[1] + later[1])


def body(inputs, x_weight, b_values, c_values, gate_z, log_decay, skip_gain, grad_out):
    token_count = inputs.shape[0]
    head_count = log_decay.shape[1]
    width_here = x_weight.shape[1]
    block_count = token_count // SPAN
    full_weight = lax.all_gather(x_weight, "seq", axis=0, tiled=True)
    x_sums = jnp.dot(inputs, full_weight, preferred_element_type=jnp.float32)
    x_values = x_sums.astype(jnp.bfloat16)
    first_head = lax.axis_index("head") * head_count
    owners = (first_head + jnp.arange(head_count)) // (HEADS // GROUPS)
    picker = (owners[:, None] == jnp.arange(GROUPS)[None, :]).astype(jnp.bfloat16)
    b_heads = jnp.einsum(
        "tgn,hg->thn", b_values, picker, preferred_element_type=jnp.float32
    ).astype(jnp.bfloat16)
    c_heads = jnp.einsum(
        "tgn,hg->thn", c_values, picker, preferred_element_type=jnp.float32
    ).astype(jnp.bfloat16)
    x_blocks = x_values.reshape(block_count, SPAN, head_count, HEAD_DIM)
    b_blocks = b_heads.reshape(block_count, SPAN, head_count, STATE)
    c_blocks = c_heads.reshape(block_count, SPAN, head_count, STATE)
    prefix = jnp.cumsum(log_decay.reshape(block_count, SPAN, head_count), axis=1)
    totals = prefix[:, -1, :]
    gate = gate_z.astype(jnp.float32).reshape(token_count, head_count, HEAD_DIM)
    upstream = grad_out.astype(jnp.float32).reshape(token_count, head_count, HEAD_DIM)
    sigma = jax.nn.sigmoid(gate)
    y_grad = upstream * gate * sigma
    grad_blocks = y_grad.reshape(block_count, SPAN, head_count, HEAD_DIM)
    low_blocks = grad_blocks.astype(jnp.bfloat16)
    tails = jnp.exp(totals[:, None, :] - prefix)
    fresh_states = jnp.einsum(
        "kshp,kshn->khpn",
        x_blocks.astype(jnp.float32) * tails[..., None],
        b_blocks.astype(jnp.float32),
        precision=EXACT_MODE,
    )
    fresh_grads = jnp.einsum(
        "kthp,kthn->khpn",
        grad_blocks * jnp.exp(prefix)[..., None],
        c_blocks.astype(jnp.float32),
        precision=EXACT_MODE,
    )
    running = jnp.cumsum(totals, axis=0)
    after = running[-1][None, :] - running
    before = running - totals
    device_decay = jnp.exp(running[-1])
    device_state = jnp.einsum("kh,khpn->hpn", jnp.exp(after), fresh_states, precision=EXACT_MODE)
    device_grad = jnp.einsum("kh,khpn->hpn", jnp.exp(before), fresh_grads, precision=EXACT_MODE)
    unit_decay = jnp.ones((head_count,), jnp.float32)
    start_state = prefix_2(
        (device_decay, device_state), "seq", compose, (unit_decay, jnp.zeros_like(device_state))
    )[1]
    end_grad = entering(
        (device_decay, device_grad), "seq", compose, (unit_decay, jnp.zeros_like(device_grad))
    )[1]
    gain = skip_gain[None, :, None]

    def forward(state, items):
        x_block, b_block, c_block, prefix_block, fresh = items
        weights = decayed_scores(c_block, b_block, prefix_block)
        local = jnp.einsum("hts,shp->thp", weights, x_block, preferred_element_type=jnp.float32)
        carried = jnp.exp(prefix_block)[:, :, None] * jnp.einsum(
            "thn,hpn->thp", c_block.astype(jnp.float32), state, precision=EXACT_MODE
        )
        state = jnp.exp(prefix_block[-1])[:, None, None] * state + fresh
        return (state, (local + carried + gain * x_block.astype(jnp.float32), weights))

    final_state, (outputs, weight_blocks) = lax.scan(
        forward, start_state, (x_blocks, b_blocks, c_blocks, prefix, fresh_states)
    )
    outputs = outputs.reshape(token_count, head_count, HEAD_DIM)
    z_grad = (upstream * outputs * sigma * (1.0 + gate * (1.0 - sigma))).astype(jnp.bfloat16)
    z_grad = z_grad.reshape(token_count, width_here)

    def backward(carry, items):
        weights, b_block, tail_block, total_block, grad_block, low_block, fresh = items
        local = jnp.einsum("hts,thp->shp", weights, low_block, preferred_element_type=jnp.float32)
        carried = tail_block[:, :, None] * jnp.einsum(
            "shn,hpn->shp", b_block.astype(jnp.float32), carry, precision=EXACT_MODE
        )
        carry = jnp.exp(total_block)[:, None, None] * carry + fresh
        return (carry, local + carried + gain * grad_block)

    final_grad, x_grads = lax.scan(
        backward,
        end_grad,
        (weight_blocks, b_blocks, tails, totals, grad_blocks, low_blocks, fresh_grads),
        reverse=True,
    )
    x_grad = x_grads.reshape(token_count, width_here).astype(jnp.bfloat16)
    partial_sums = jnp.einsum("tk,dk->td", x_grad, full_weight, preferred_element_type=jnp.float32)
    input_grad = lax.psum_scatter(
        partial_sums.astype(jnp.bfloat16), "head", scatter_dimension=1, tiled=True
    )
    return (input_grad, z_grad)


SEQ = 8
RUNS = 4
F32 = jnp.float32
BF16 = jnp.bfloat16


def dot_nn(a, b):
    return lax.dot_general(a, b, (((1,), (0,)), ((), ())), preferred_element_type=F32)


def dot_nt(a, b):
    return lax.dot_general(a, b, (((1,), (1,)), ((), ())), preferred_element_type=F32)


def dot_tn(a, b):
    return lax.dot_general(a, b, (((0,), (0,)), ((), ())), preferred_element_type=F32)


def mixer_kernel(
    in_hbm, w_hbm, b_flat, c_flat, gz_hbm, go_hbm, decay_ref, skip_ref,
    out_ref, zg_ref,
    inputs, gz, go, b2, c2, pexp, prow, gain, tt,
    wbuf, xacc, xg, xg16, ysc, wts, gmat, x16, pbuf, rin, rdir,
    fbuf, rf, sb, rr, rt,
    loads, wsend, wrecv, wlocal, tsend, trecv, esend, erecv, rsend, rrecv, rdrecv,
):
    s = lax.axis_index("seq")
    z = lax.axis_index("head")
    core, xx, yy = s % 2, (s // 2) % 2, s // 4
    half = w_hbm.shape[1]
    heads = wts.shape[0]
    pairs = heads // 2
    per_group = pairs // b2.shape[0]

    def peer(r):
        a = (1 - core) if r & 1 else core
        b = (1 - xx) if r & 2 else xx
        c = (1 - yy) if r & 4 else yy
        return c * 4 + b * 2 + a

    def peer_dyn(r):
        a = (core + r) % 2
        b = (xx + r // 2) % 2
        c = (yy + r // 4) % 2
        return c * 4 + b * 2 + a

    staged = [pltpu.make_async_copy(src, dst, loads.at[n]) for n, (src, dst) in enumerate(
        ((gz_hbm, gz), (go_hbm, go), (in_hbm, inputs)))]
    for cp in staged:
        cp.start()
    barrier = pltpu.get_barrier_semaphore()
    for r in range(1, SEQ):
        pl.semaphore_signal(barrier, inc=1, device_id={"seq": peer(r)}, device_id_type=pl.DeviceIdType.MESH)
    for dz in range(1, RUNS):
        pl.semaphore_signal(barrier, inc=1, device_id={"head": (z + dz) % RUNS}, device_id_type=pl.DeviceIdType.MESH)
    pl.semaphore_wait(barrier, SEQ - 1 + RUNS - 1)

    def wcopy(src_slot, dst_slot, h, to):
        src = w_hbm.at[h] if src_slot == 0 else wbuf.at[src_slot, h]
        return pltpu.make_async_remote_copy(
            src_ref=src, dst_ref=wbuf.at[dst_slot, h],
            send_sem=wsend.at[dst_slot, h], recv_sem=wrecv.at[dst_slot, h],
            device_id={"seq": peer(to)}, device_id_type=pl.DeviceIdType.MESH)

    own = pltpu.make_async_copy(w_hbm, wbuf.at[0], wlocal)
    sent = []

    def go_send(src_slot, dst_slot, h, to):
        cp = wcopy(src_slot, dst_slot, h, to)
        cp.start()
        sent.append(cp)

    def w_wait(slot, h, to):
        wcopy(0, slot, h, to).wait_recv()

    def tcopy(r, slot):
        k = peer(r)
        return pltpu.make_async_remote_copy(
            src_ref=tt.at[k], dst_ref=rt.at[slot], send_sem=tsend.at[r], recv_sem=trecv.at[slot],
            device_id={"seq": k}, device_id_type=pl.DeviceIdType.MESH)

    go_send(0, 2, 0, 2)
    go_send(0, 4, 1, 4)
    go_send(0, 2, 1, 2)
    go_send(0, 4, 0, 4)
    own.start()
    go_send(0, 1, 0, 1)
    go_send(0, 1, 1, 1)

    groups = b2.shape[0]
    for g in range(groups):
        span = pl.ds(pl.multiple_of((z * groups + g) * STATE, STATE), STATE)
        b2[g] = b_flat[:, span]
        c2[g] = c_flat[:, span]
    lower = (lax.broadcasted_iota(jnp.int32, (SPAN, SPAN), 0) >= lax.broadcasted_iota(jnp.int32, (SPAN, SPAN), 1))
    ones = jnp.where(lower, 1.0, 0.0).astype(F32)
    prefix = lax.dot_general(ones, decay_ref[...], (((1,), (0,)), ((), ())), preferred_element_type=F32, precision=EXACT_MODE)
    across = lax.dot_general(decay_ref[...], ones, (((0,), (1,)), ((), ())), preferred_element_type=F32, precision=EXACT_MODE)
    per_chunk = heads // SEQ
    closing = jnp.broadcast_to(across[:, SPAN - 1:SPAN], (heads, 128))
    tt[...] = jnp.zeros_like(tt)
    for j in range(SEQ):
        tt[j, 0:per_chunk, :] = closing[j * per_chunk:(j + 1) * per_chunk, :]
    for i in range(pairs):
        prow[i, 0:2, :] = across[2 * i:2 * i + 2, :]
    both = jnp.concatenate([prefix, jnp.broadcast_to(skip_ref[...], (8, heads))], axis=0)

    def expand_pair(i, carry):
        head = lax.broadcasted_iota(jnp.int32, (heads, 128), 0)
        lane = lax.broadcasted_iota(jnp.int32, (heads, 128), 1)
        pick = jnp.where(head == 2 * i + lane // HEAD_DIM, 1.0, 0.0).astype(F32)
        wide = lax.dot_general(both, pick, (((1,), (0,)), ((), ())), preferred_element_type=F32, precision=EXACT_MODE)
        pexp[i] = wide[:SPAN]
        gain[i] = wide[SPAN:]
        return carry

    lax.fori_loop(0, pairs, expand_pair, 0)
    rt[s] = tt[s]
    for r in range(1, SEQ):
        tcopy(r, s).start()
    staged[0].wait()
    staged[1].wait()
    for g in range(groups):
        gmat[g] = dot_nt(c2[g], b2[g])
    xacc[...] = jnp.zeros_like(xacc)
    lanes = lax.broadcasted_iota(jnp.int32, (SPAN, 128), 1)
    left = lanes < HEAD_DIM
    causal = lax.broadcasted_iota(jnp.int32, (SPAN, SPAN), 0) >= lax.broadcasted_iota(jnp.int32, (SPAN, SPAN), 1)

    def columns_of(i):
        return pl.ds(pl.multiple_of(i * 128, 128), 128)

    def back_pair(i, carry):
        cols = columns_of(i)
        gate = gz[:, cols].astype(F32)
        up = go[:, cols].astype(F32)
        grad = up * gate * jax.nn.sigmoid(gate)
        low = grad.astype(BF16)
        pe = pexp[i]
        ysc[:, cols] = (grad * jnp.exp(pe)).astype(BF16)
        scores = gmat[i // per_group]
        acc = []
        for k in range(2):
            later = pe[:, HEAD_DIM * k:HEAD_DIM * k + 1]
            earlier = prow[i, k:k + 1, :]
            factors = jnp.exp(jnp.where(causal, later - earlier, -1e30))
            w = (scores * factors).astype(BF16)
            wts[2 * i + k] = w
            acc.append(dot_tn(w, low))
        xg[:, cols] = jnp.where(left, acc[0], acc[1]) + gain[i, 0:1, :] * grad
        return carry

    lax.fori_loop(0, pairs, back_pair, 0)

    def ecopy(e, f, r, slot):
        k = peer(r)
        src, dst = (fbuf, rf) if f == 0 else (sb, rr)
        return pltpu.make_async_remote_copy(
            src_ref=src.at[e, k], dst_ref=dst.at[e, slot],
            send_sem=esend.at[e, f, r], recv_sem=erecv.at[e, f, slot],
            device_id={"seq": k}, device_id_type=pl.DeviceIdType.MESH)

    def e_start(e, f):
        for r in range(1, SEQ):
            ecopy(e, f, r, s).start()
        if f == 0:
            rf[e, s] = fbuf[e, s]
        else:
            rr[e, s] = sb[e, s]

    def e_wait(e, f):
        for r in range(1, SEQ):
            ecopy(e, f, r, peer(r)).wait_recv()

    def fresh(e, src, maps):
        def one(j, carry):
            cols = pl.ds(pl.multiple_of(j * 256, 256), 256)
            fbuf[e, j] = dot_tn(src[:, cols], maps[j // (SEQ // b2.shape[0])]).astype(BF16)
            return carry

        lax.fori_loop(0, SEQ, one, 0)

    def scan_states(e, order):
        per = heads // SEQ
        run = [jnp.zeros((HEAD_DIM, STATE), F32) for _ in range(per)]
        for k in order:
            decay = jnp.exp(rt[k])
            for m in range(per):
                rows = slice(m * HEAD_DIM, (m + 1) * HEAD_DIM)
                sb[e, k, rows, :] = run[m].astype(BF16)
                run[m] = run[m] * decay[m:m + 1, :] + rf[e, k, rows, :].astype(F32)

    def x_part(first, count):
        def one(i, carry):
            slot, h = i // 2, i % 2
            start = peer_dyn(slot) * 2 * half + h * half
            a = inputs[:, pl.ds(pl.multiple_of(start, 256), half)]
            for q in range(4):
                cs = slice(q * 512, (q + 1) * 512)
                xacc[:, cs] += dot_nn(a, wbuf[slot, h, :, cs])
            return carry

        lax.fori_loop(first, first + count, one, 0)

    def route(i):
        target = peer_dyn(i // 2) // 2
        up = (z + RUNS - 1 - target) // RUNS
        return target, up, up * (RUNS - 1)

    def rcopy(i, up):
        return pltpu.make_async_remote_copy(
            src_ref=pbuf.at[i], dst_ref=rin.at[up, i - 12],
            send_sem=rsend.at[i], recv_sem=rrecv.at[up, i - 12],
            device_id={"head": (z + 1 + up * 2) % RUNS}, device_id_type=pl.DeviceIdType.MESH)

    def dcopy(i, source, target):
        return pltpu.make_async_remote_copy(
            src_ref=pbuf.at[i], dst_ref=rdir.at[source, i % 4],
            send_sem=rsend.at[i], recv_sem=rdrecv.at[source, i % 4],
            device_id={"head": target}, device_id_type=pl.DeviceIdType.MESH)

    def p_part(first, count):
        def one(i, carry):
            slot, h = i // 2, i % 2
            target, up, edge = route(i)
            pbuf[i] = dot_nt(xg16[...], wbuf[slot, h]).astype(BF16)
            if first >= 12:
                @pl.when((target != z) & (z == edge))
                def _():
                    rcopy(i, up).start()
            else:
                @pl.when(target != z)
                def _():
                    dcopy(i, z, target).start()

            return carry

        lax.fori_loop(first, first + count, one, 0)

    def p_pass(first, count):
        def one(i, carry):
            target, up, edge = route(i)

            @pl.when((target != z) & (z != edge))
            def _():
                rcopy(i, up).wait_recv()
                pbuf[i] = (pbuf[i].astype(F32) + rin[up, i - 12].astype(F32)).astype(BF16)
                rcopy(i, up).start()

            return carry

        lax.fori_loop(first, first + count, one, 0)

    fresh(0, ysc, c2)
    e_start(0, 0)
    own.wait()
    staged[2].wait()
    x_part(0, 2)
    for r in range(1, SEQ):
        tcopy(r, peer(r)).wait_recv()
    e_wait(0, 0)
    scan_states(0, range(SEQ - 1, -1, -1))
    e_start(0, 1)
    w_wait(1, 0, 1)
    w_wait(1, 1, 1)
    x_part(2, 2)
    e_wait(0, 1)

    def back_finish(i, carry):
        cols = columns_of(i)
        state = rr[0, i // 2, pl.ds(pl.multiple_of((i % 2) * 128, 128), 128), :]
        pe = pexp[i]
        tail = jnp.exp(pe[SPAN - 1:SPAN, :] - pe)
        xg16[:, cols] = (xg[:, cols] + tail * dot_nt(b2[i // per_group], state)).astype(BF16)
        return carry

    lax.fori_loop(0, pairs, back_finish, 0)
    w_wait(2, 0, 2)
    go_send(2, 6, 0, 4)
    go_send(2, 3, 0, 1)
    w_wait(4, 1, 4)
    go_send(4, 6, 1, 2)
    go_send(4, 5, 1, 1)
    p_part(0, 4)
    w_wait(2, 1, 2)
    go_send(2, 3, 1, 1)
    w_wait(4, 0, 4)
    go_send(4, 5, 0, 1)
    x_part(4, 2)
    p_part(4, 2)
    x_part(8, 2)
    p_part(8, 2)
    for h in range(2):
        w_wait(3, h, 1)
        w_wait(5, h, 1)
    x_part(6, 2)
    p_part(6, 2)
    x_part(10, 2)
    p_part(10, 2)
    w_wait(6, 0, 4)
    go_send(6, 7, 0, 1)
    w_wait(6, 1, 2)
    go_send(6, 7, 1, 1)
    x_part(12, 2)
    p_part(12, 2)
    w_wait(7, 0, 1)
    w_wait(7, 1, 1)
    x_part(14, 2)

    def fore_scale(i, carry):
        cols = columns_of(i)
        x = xacc[:, cols].astype(BF16)
        x16[:, cols] = x
        pe = pexp[i]
        ysc[:, cols] = (x.astype(F32) * jnp.exp(pe[SPAN - 1:SPAN, :] - pe)).astype(BF16)
        return carry

    lax.fori_loop(0, pairs, fore_scale, 0)
    fresh(1, ysc, b2)
    e_start(1, 0)
    p_part(14, 2)
    p_pass(12, 2)
    e_wait(1, 0)
    scan_states(1, range(SEQ))
    e_start(1, 1)
    p_pass(14, 2)

    def fore_local(i, carry):
        cols = columns_of(i)
        x = x16[:, cols]
        y = jnp.where(left, dot_nn(wts[2 * i], x), dot_nn(wts[2 * i + 1], x))
        xacc[:, cols] = y + gain[i, 0:1, :] * x.astype(F32)
        return carry

    lax.fori_loop(0, pairs, fore_local, 0)
    e_wait(1, 1)

    def fore_finish(i, carry):
        cols = columns_of(i)
        state = rr[1, i // 2, pl.ds(pl.multiple_of((i % 2) * 128, 128), 128), :]
        y = xacc[:, cols] + jnp.exp(pexp[i]) * dot_nt(c2[i // per_group], state)
        gate = gz[:, cols].astype(F32)
        up = go[:, cols].astype(F32)
        sigma = jax.nn.sigmoid(gate)
        zg_ref[:, cols] = (up * y * sigma * (1.0 + gate * (1.0 - sigma))).astype(BF16)
        return carry

    lax.fori_loop(0, pairs, fore_finish, 0)

    def own_chunk(i, far):
        owner = peer_dyn(i // 2)

        @pl.when(owner // 2 == z)
        def _():
            piece = (owner % 2) * 2 + i % 2
            out_cols = pl.ds(pl.multiple_of(piece * 256, 256), 256)
            xg[:, out_cols] = pbuf[i].astype(F32)
            if far:
                @pl.when(z != 0)
                def _():
                    rcopy(i, 0).wait_recv()
                    xg[:, out_cols] += rin[0, i - 12].astype(F32)

                @pl.when(z != RUNS - 1)
                def _():
                    rcopy(i, 1).wait_recv()
                    xg[:, out_cols] += rin[1, i - 12].astype(F32)
            else:
                for dz in range(1, RUNS):
                    source = (z + dz) % RUNS
                    dcopy(i, source, source).wait_recv()
                    xg[:, out_cols] += rdir[source, i % 4].astype(F32)
            out_ref[:, out_cols] = xg[:, out_cols].astype(BF16)

    def own_near(i, carry):
        own_chunk(i, False)
        return carry

    def own_far(i, carry):
        own_chunk(i, True)
        return carry

    lax.fori_loop(0, 12, own_near, 0)
    lax.fori_loop(12, 16, own_far, 0)

    def drain(i, carry):
        target = route(i)[0]

        @pl.when(target != z)
        def _():
            dcopy(i, z, target).wait_send()

        return carry

    lax.fori_loop(0, 16, drain, 0)
    for cp in sent:
        cp.wait_send()
    for r in range(1, SEQ):
        tcopy(r, s).wait_send()
        for e in range(2):
            for f in range(2):
                ecopy(e, f, r, s).wait_send()


def fused_body(inputs, x_weight, b_values, c_values, gate_z, log_decay, skip_gain, grad_out):
    heads = log_decay.shape[1]
    width = x_weight.shape[1]
    depth = x_weight.shape[0]
    pairs = heads // 2
    groups = heads * GROUPS // HEADS
    b_flat = b_values.reshape(b_values.shape[0], GROUPS * STATE)
    c_flat = c_values.reshape(c_values.shape[0], GROUPS * STATE)
    halves = x_weight.reshape(2, depth // 2, width)
    vmem = pl.BlockSpec(memory_space=pltpu.VMEM)
    hbm = pl.BlockSpec(memory_space=pl.ANY)
    tokens = inputs.shape[0]
    dma = pltpu.SemaphoreType.DMA
    state = (2, SEQ, heads // SEQ * HEAD_DIM, STATE)
    return tuple(pl.pallas_call(
        mixer_kernel,
        out_shape=(
            jax.ShapeDtypeStruct((tokens, inputs.shape[1] // RUNS), BF16),
            jax.ShapeDtypeStruct((tokens, width), BF16),
        ),
        in_specs=[hbm, hbm, vmem, vmem, hbm, hbm, vmem, vmem],
        out_specs=(vmem, vmem),
        scratch_shapes=[
            pltpu.VMEM(inputs.shape, BF16),
            pltpu.VMEM((tokens, width), BF16),
            pltpu.VMEM((tokens, width), BF16),
            pltpu.VMEM((groups, SPAN, STATE), BF16),
            pltpu.VMEM((groups, SPAN, STATE), BF16),
            pltpu.VMEM((pairs, SPAN, 128), F32),
            pltpu.VMEM((pairs, 8, SPAN), F32),
            pltpu.VMEM((pairs, 8, 128), F32),
            pltpu.VMEM((SEQ, 8, 128), F32),
            pltpu.VMEM((SEQ, 2, depth // 2, width), BF16),
            pltpu.VMEM((tokens, width), F32),
            pltpu.VMEM((tokens, width), F32),
            pltpu.VMEM((tokens, width), BF16),
            pltpu.VMEM((tokens, width), BF16),
            pltpu.VMEM((heads, SPAN, SPAN), BF16),
            pltpu.VMEM((groups, SPAN, SPAN), F32),
            pltpu.VMEM((tokens, width), BF16),
            pltpu.VMEM((2 * SEQ, tokens, depth // 2), BF16),
            pltpu.VMEM((2, 4, tokens, depth // 2), BF16),
            pltpu.VMEM((RUNS, 4, tokens, depth // 2), BF16),
            pltpu.VMEM(state, BF16),
            pltpu.VMEM(state, BF16),
            pltpu.VMEM(state, BF16),
            pltpu.VMEM(state, BF16),
            pltpu.VMEM((SEQ, 8, 128), F32),
            dma((3,)), dma((SEQ, 2)), dma((SEQ, 2)), dma,
            dma((SEQ,)), dma((SEQ,)),
            dma((2, 2, SEQ)), dma((2, 2, SEQ)),
            dma((2 * SEQ,)), dma((2, 4)), dma((RUNS, 4)),
        ],
        compiler_params=pltpu.CompilerParams(
            collective_id=0, has_side_effects=True, vmem_limit_bytes=60 * 1024 * 1024),
        name="mixer",
    )(inputs, halves, b_flat, c_flat, gate_z, grad_out, log_decay, skip_gain[None, :]))


def solution(mesh):
    in_specs = (
        P("seq", None),
        P("seq", "head"),
        P("seq", None, None),
        P("seq", None, None),
        P("seq", "head"),
        P("seq", "head"),
        P("head"),
        P("seq", "head"),
    )
    out_specs = (P("seq", "head"), P("seq", "head"))
    small = mesh.shape["seq"] == SEQ and mesh.shape["head"] == RUNS
    chosen = fused_body if small else body
    return jax.shard_map(chosen, mesh=mesh, in_specs=in_specs, out_specs=out_specs, check_vma=False)
```

```python
import jax
import jax.numpy as jnp
from jax import lax
from jax.sharding import PartitionSpec as P
from jax.experimental import pallas as pl
from jax.experimental.pallas import tpu as pltpu

HEADS = 128
HEAD_DIM = 64
STATE = 128
GROUPS = 8
SPAN = 256


EXACT_MODE = lax.Precision.HIGHEST


def prefix_2(array, axis, combine, identity):
    size, place = (lax.axis_size(axis), lax.axis_index(axis))
    everything = jax.tree.map(
        lambda part, kind: lax.all_gather(part.astype(kind), axis),
        array,
        (jnp.bfloat16, jnp.bfloat16),
    )
    start = jax.tree.map(
        lambda part, zero: jnp.broadcast_to(jnp.asarray(zero, part.dtype), part.shape),
        array,
        identity,
    )

    def prefix_hop(k, before):
        reached = k < place
        new = combine(
            before, jax.tree.map(lambda part, own: part[k].astype(own.dtype), everything, array)
        )
        return jax.tree.map(lambda a, b: jnp.where(reached, a, b), new, before)

    return lax.fori_loop(0, size, prefix_hop, start)


def entering(value, axis, join, neutral):
    count, mine = (lax.axis_size(axis), lax.axis_index(axis))
    pieces = jax.tree.map(lambda part: lax.all_gather(part, axis), value)
    pieces = jax.tree.map(lambda part: part[::-1], pieces)
    mine = count - 1 - mine
    so_far = jax.tree.map(
        lambda part, zero: jnp.full_like(part, 0) + jnp.asarray(zero, part.dtype), value, neutral
    )

    def entering_hop(position, so_far):
        longer = join(so_far, jax.tree.map(lambda part: part[position], pieces))
        return jax.tree.map(lambda new, old: jnp.where(position < mine, new, old), longer, so_far)

    return lax.fori_loop(0, count - 1, entering_hop, so_far)


def decayed_scores(c_block, b_block, prefix):
    scores = jnp.einsum("thn,shn->hts", c_block, b_block, preferred_element_type=jnp.float32)
    later = prefix.T[:, :, None]
    earlier = prefix.T[:, None, :]
    positions = jnp.arange(prefix.shape[0])
    causal = (positions[:, None] >= positions[None, :])[None, :, :]
    spacing = jnp.where(causal, later - earlier, 0.0)
    factors = jnp.where(causal, jnp.exp(spacing), 0.0)
    return (scores * factors).astype(jnp.bfloat16)


def compose(earlier, later):
    return (earlier[0] * later[0], later[0][:, None, None] * earlier[1] + later[1])


def body(inputs, x_weight, b_values, c_values, gate_z, log_decay, skip_gain, grad_out):
    token_count = inputs.shape[0]
    head_count = log_decay.shape[1]
    width_here = x_weight.shape[1]
    block_count = token_count // SPAN
    full_weight = lax.all_gather(x_weight, "seq", axis=0, tiled=True)
    x_sums = jnp.dot(inputs, full_weight, preferred_element_type=jnp.float32)
    x_values = x_sums.astype(jnp.bfloat16)
    first_head = lax.axis_index("head") * head_count
    owners = (first_head + jnp.arange(head_count)) // (HEADS // GROUPS)
    picker = (owners[:, None] == jnp.arange(GROUPS)[None, :]).astype(jnp.bfloat16)
    b_heads = jnp.einsum(
        "tgn,hg->thn", b_values, picker, preferred_element_type=jnp.float32
    ).astype(jnp.bfloat16)
    c_heads = jnp.einsum(
        "tgn,hg->thn", c_values, picker, preferred_element_type=jnp.float32
    ).astype(jnp.bfloat16)
    x_blocks = x_values.reshape(block_count, SPAN, head_count, HEAD_DIM)
    b_blocks = b_heads.reshape(block_count, SPAN, head_count, STATE)
    c_blocks = c_heads.reshape(block_count, SPAN, head_count, STATE)
    prefix = jnp.cumsum(log_decay.reshape(block_count, SPAN, head_count), axis=1)
    totals = prefix[:, -1, :]
    gate = gate_z.astype(jnp.float32).reshape(token_count, head_count, HEAD_DIM)
    upstream = grad_out.astype(jnp.float32).reshape(token_count, head_count, HEAD_DIM)
    sigma = jax.nn.sigmoid(gate)
    y_grad = upstream * gate * sigma
    grad_blocks = y_grad.reshape(block_count, SPAN, head_count, HEAD_DIM)
    low_blocks = grad_blocks.astype(jnp.bfloat16)
    tails = jnp.exp(totals[:, None, :] - prefix)
    fresh_states = jnp.einsum(
        "kshp,kshn->khpn",
        x_blocks.astype(jnp.float32) * tails[..., None],
        b_blocks.astype(jnp.float32),
        precision=EXACT_MODE,
    )
    fresh_grads = jnp.einsum(
        "kthp,kthn->khpn",
        grad_blocks * jnp.exp(prefix)[..., None],
        c_blocks.astype(jnp.float32),
        precision=EXACT_MODE,
    )
    running = jnp.cumsum(totals, axis=0)
    after = running[-1][None, :] - running
    before = running - totals
    device_decay = jnp.exp(running[-1])
    device_state = jnp.einsum("kh,khpn->hpn", jnp.exp(after), fresh_states, precision=EXACT_MODE)
    device_grad = jnp.einsum("kh,khpn->hpn", jnp.exp(before), fresh_grads, precision=EXACT_MODE)
    unit_decay = jnp.ones((head_count,), jnp.float32)
    start_state = prefix_2(
        (device_decay, device_state), "seq", compose, (unit_decay, jnp.zeros_like(device_state))
    )[1]
    end_grad = entering(
        (device_decay, device_grad), "seq", compose, (unit_decay, jnp.zeros_like(device_grad))
    )[1]
    gain = skip_gain[None, :, None]

    def forward(state, items):
        x_block, b_block, c_block, prefix_block, fresh = items
        weights = decayed_scores(c_block, b_block, prefix_block)
        local = jnp.einsum("hts,shp->thp", weights, x_block, preferred_element_type=jnp.float32)
        carried = jnp.exp(prefix_block)[:, :, None] * jnp.einsum(
            "thn,hpn->thp", c_block.astype(jnp.float32), state, precision=EXACT_MODE
        )
        state = jnp.exp(prefix_block[-1])[:, None, None] * state + fresh
        return (state, (local + carried + gain * x_block.astype(jnp.float32), weights))

    final_state, (outputs, weight_blocks) = lax.scan(
        forward, start_state, (x_blocks, b_blocks, c_blocks, prefix, fresh_states)
    )
    outputs = outputs.reshape(token_count, head_count, HEAD_DIM)
    z_grad = (upstream * outputs * sigma * (1.0 + gate * (1.0 - sigma))).astype(jnp.bfloat16)
    z_grad = z_grad.reshape(token_count, width_here)

    def backward(carry, items):
        weights, b_block, tail_block, total_block, grad_block, low_block, fresh = items
        local = jnp.einsum("hts,thp->shp", weights, low_block, preferred_element_type=jnp.float32)
        carried = tail_block[:, :, None] * jnp.einsum(
            "shn,hpn->shp", b_block.astype(jnp.float32), carry, precision=EXACT_MODE
        )
        carry = jnp.exp(total_block)[:, None, None] * carry + fresh
        return (carry, local + carried + gain * grad_block)

    final_grad, x_grads = lax.scan(
        backward,
        end_grad,
        (weight_blocks, b_blocks, tails, totals, grad_blocks, low_blocks, fresh_grads),
        reverse=True,
    )
    x_grad = x_grads.reshape(token_count, width_here).astype(jnp.bfloat16)
    partial_sums = jnp.einsum("tk,dk->td", x_grad, full_weight, preferred_element_type=jnp.float32)
    input_grad = lax.psum_scatter(
        partial_sums.astype(jnp.bfloat16), "head", scatter_dimension=1, tiled=True
    )
    return (input_grad, z_grad)


SEQ = 8
RUNS = 4
F32 = jnp.float32
BF16 = jnp.bfloat16


def dot_nn(a, b):
    return lax.dot_general(a, b, (((1,), (0,)), ((), ())), preferred_element_type=F32)


def dot_nt(a, b):
    return lax.dot_general(a, b, (((1,), (1,)), ((), ())), preferred_element_type=F32)


def dot_tn(a, b):
    return lax.dot_general(a, b, (((0,), (0,)), ((), ())), preferred_element_type=F32)


def mixer_kernel(
    in_hbm, w_hbm, b_flat, c_flat, gz_hbm, go_hbm, decay_ref, skip_ref,
    out_ref, zg_ref,
    inputs, gz, go, b2, c2, pexp, prow, gain, tt,
    wbuf, xacc, xg, xg16, ysc, wts, gmat, x16, pbuf, rin, rdir,
    fbuf, rf, sb, rr, rt,
    loads, wsend, wrecv, wlocal, tsend, trecv, esend, erecv, rsend, rrecv, rdrecv,
):
    s = lax.axis_index("seq")
    z = lax.axis_index("head")
    core, xx, yy = s % 2, (s // 2) % 2, s // 4
    half = w_hbm.shape[1]
    heads = wts.shape[0]
    pairs = heads // 2
    per_group = pairs // b2.shape[0]

    def peer(r):
        a = (1 - core) if r & 1 else core
        b = (1 - xx) if r & 2 else xx
        c = (1 - yy) if r & 4 else yy
        return c * 4 + b * 2 + a

    def peer_dyn(r):
        a = (core + r) % 2
        b = (xx + r // 2) % 2
        c = (yy + r // 4) % 2
        return c * 4 + b * 2 + a

    staged = [pltpu.make_async_copy(src, dst, loads.at[n]) for n, (src, dst) in enumerate(
        ((gz_hbm, gz), (go_hbm, go), (in_hbm, inputs)))]
    for cp in staged:
        cp.start()
    barrier = pltpu.get_barrier_semaphore()
    for r in range(1, SEQ):
        pl.semaphore_signal(barrier, inc=1, device_id={"seq": peer(r)}, device_id_type=pl.DeviceIdType.MESH)
    for dz in range(1, RUNS):
        pl.semaphore_signal(barrier, inc=1, device_id={"head": (z + dz) % RUNS}, device_id_type=pl.DeviceIdType.MESH)
    pl.semaphore_wait(barrier, SEQ - 1 + RUNS - 1)

    def wcopy(src_slot, dst_slot, h, to):
        src = w_hbm.at[h] if src_slot == 0 else wbuf.at[src_slot, h]
        return pltpu.make_async_remote_copy(
            src_ref=src, dst_ref=wbuf.at[dst_slot, h],
            send_sem=wsend.at[dst_slot, h], recv_sem=wrecv.at[dst_slot, h],
            device_id={"seq": peer(to)}, device_id_type=pl.DeviceIdType.MESH)

    own = pltpu.make_async_copy(w_hbm, wbuf.at[0], wlocal)
    sent = []

    def go_send(src_slot, dst_slot, h, to):
        cp = wcopy(src_slot, dst_slot, h, to)
        cp.start()
        sent.append(cp)

    def w_wait(slot, h, to):
        wcopy(0, slot, h, to).wait_recv()

    def tcopy(r, slot):
        k = peer(r)
        return pltpu.make_async_remote_copy(
            src_ref=tt.at[k], dst_ref=rt.at[slot], send_sem=tsend.at[r], recv_sem=trecv.at[slot],
            device_id={"seq": k}, device_id_type=pl.DeviceIdType.MESH)

    go_send(0, 2, 0, 2)
    go_send(0, 4, 1, 4)
    go_send(0, 2, 1, 2)
    go_send(0, 4, 0, 4)
    own.start()
    go_send(0, 1, 0, 1)
    go_send(0, 1, 1, 1)

    groups = b2.shape[0]
    for g in range(groups):
        span = pl.ds(pl.multiple_of((z * groups + g) * STATE, STATE), STATE)
        b2[g] = b_flat[:, span]
        c2[g] = c_flat[:, span]
    lower = (lax.broadcasted_iota(jnp.int32, (SPAN, SPAN), 0) >= lax.broadcasted_iota(jnp.int32, (SPAN, SPAN), 1))
    ones = jnp.where(lower, 1.0, 0.0).astype(F32)
    prefix = lax.dot_general(ones, decay_ref[...], (((1,), (0,)), ((), ())), preferred_element_type=F32, precision=EXACT_MODE)
    across = lax.dot_general(decay_ref[...], ones, (((0,), (1,)), ((), ())), preferred_element_type=F32, precision=EXACT_MODE)
    per_chunk = heads // SEQ
    closing = jnp.broadcast_to(across[:, SPAN - 1:SPAN], (heads, 128))
    tt[...] = jnp.zeros_like(tt)
    for j in range(SEQ):
        tt[j, 0:per_chunk, :] = closing[j * per_chunk:(j + 1) * per_chunk, :]
    for i in range(pairs):
        prow[i, 0:2, :] = across[2 * i:2 * i + 2, :]
    both = jnp.concatenate([prefix, jnp.broadcast_to(skip_ref[...], (8, heads))], axis=0)

    def expand_pair(i, carry):
        head = lax.broadcasted_iota(jnp.int32, (heads, 128), 0)
        lane = lax.broadcasted_iota(jnp.int32, (heads, 128), 1)
        pick = jnp.where(head == 2 * i + lane // HEAD_DIM, 1.0, 0.0).astype(F32)
        wide = lax.dot_general(both, pick, (((1,), (0,)), ((), ())), preferred_element_type=F32, precision=EXACT_MODE)
        pexp[i] = wide[:SPAN]
        gain[i] = wide[SPAN:]
        return carry

    lax.fori_loop(0, pairs, expand_pair, 0)
    rt[s] = tt[s]
    for r in range(1, SEQ):
        tcopy(r, s).start()
    staged[0].wait()
    staged[1].wait()
    for g in range(groups):
        gmat[g] = dot_nt(c2[g], b2[g])
    xacc[...] = jnp.zeros_like(xacc)
    lanes = lax.broadcasted_iota(jnp.int32, (SPAN, 128), 1)
    left = lanes < HEAD_DIM
    causal = lax.broadcasted_iota(jnp.int32, (SPAN, SPAN), 0) >= lax.broadcasted_iota(jnp.int32, (SPAN, SPAN), 1)

    def columns_of(i):
        return pl.ds(pl.multiple_of(i * 128, 128), 128)

    def back_pair(i, carry):
        cols = columns_of(i)
        gate = gz[:, cols].astype(F32)
        up = go[:, cols].astype(F32)
        grad = up * gate * jax.nn.sigmoid(gate)
        low = grad.astype(BF16)
        pe = pexp[i]
        ysc[:, cols] = (grad * jnp.exp(pe)).astype(BF16)
        scores = gmat[i // per_group]
        acc = []
        for k in range(2):
            later = pe[:, HEAD_DIM * k:HEAD_DIM * k + 1]
            earlier = prow[i, k:k + 1, :]
            factors = jnp.exp(jnp.where(causal, later - earlier, -1e30))
            w = (scores * factors).astype(BF16)
            wts[2 * i + k] = w
            acc.append(dot_tn(w, low))
        xg[:, cols] = jnp.where(left, acc[0], acc[1]) + gain[i, 0:1, :] * grad
        return carry

    lax.fori_loop(0, pairs, back_pair, 0)

    def ecopy(e, f, r, slot):
        k = peer(r)
        src, dst = (fbuf, rf) if f == 0 else (sb, rr)
        return pltpu.make_async_remote_copy(
            src_ref=src.at[e, k], dst_ref=dst.at[e, slot],
            send_sem=esend.at[e, f, r], recv_sem=erecv.at[e, f, slot],
            device_id={"seq": k}, device_id_type=pl.DeviceIdType.MESH)

    def e_start(e, f):
        for r in range(1, SEQ):
            ecopy(e, f, r, s).start()
        if f == 0:
            rf[e, s] = fbuf[e, s]
        else:
            rr[e, s] = sb[e, s]

    def e_wait(e, f):
        for r in range(1, SEQ):
            ecopy(e, f, r, peer(r)).wait_recv()

    def fresh(e, src, maps):
        def one(j, carry):
            cols = pl.ds(pl.multiple_of(j * 256, 256), 256)
            fbuf[e, j] = dot_tn(src[:, cols], maps[j // (SEQ // b2.shape[0])]).astype(BF16)
            return carry

        lax.fori_loop(0, SEQ, one, 0)

    def scan_states(e, order):
        per = heads // SEQ
        run = [jnp.zeros((HEAD_DIM, STATE), F32) for _ in range(per)]
        for k in order:
            decay = jnp.exp(rt[k])
            for m in range(per):
                rows = slice(m * HEAD_DIM, (m + 1) * HEAD_DIM)
                sb[e, k, rows, :] = run[m].astype(BF16)
                run[m] = run[m] * decay[m:m + 1, :] + rf[e, k, rows, :].astype(F32)

    def x_part(first, count):
        def one(i, carry):
            slot, h = i // 2, i % 2
            start = peer_dyn(slot) * 2 * half + h * half
            a = inputs[:, pl.ds(pl.multiple_of(start, 256), half)]
            for q in range(4):
                cs = slice(q * 512, (q + 1) * 512)
                xacc[:, cs] += dot_nn(a, wbuf[slot, h, :, cs])
            return carry

        lax.fori_loop(first, first + count, one, 0)

    def route(i):
        target = peer_dyn(i // 2) // 2
        up = (z + RUNS - 1 - target) // RUNS
        return target, up, up * (RUNS - 1)

    def rcopy(i, up):
        return pltpu.make_async_remote_copy(
            src_ref=pbuf.at[i], dst_ref=rin.at[up, i - 12],
            send_sem=rsend.at[i], recv_sem=rrecv.at[up, i - 12],
            device_id={"head": (z + 1 + up * 2) % RUNS}, device_id_type=pl.DeviceIdType.MESH)

    def dcopy(i, source, target):
        return pltpu.make_async_remote_copy(
            src_ref=pbuf.at[i], dst_ref=rdir.at[source, i % 4],
            send_sem=rsend.at[i], recv_sem=rdrecv.at[source, i % 4],
            device_id={"head": target}, device_id_type=pl.DeviceIdType.MESH)

    def p_part(first, count):
        def one(i, carry):
            slot, h = i // 2, i % 2
            target, up, edge = route(i)
            pbuf[i] = dot_nt(xg16[...], wbuf[slot, h]).astype(BF16)
            if first >= 12:
                @pl.when((target != z) & (z == edge))
                def _():
                    rcopy(i, up).start()
            else:
                @pl.when(target != z)
                def _():
                    dcopy(i, z, target).start()

            return carry

        lax.fori_loop(first, first + count, one, 0)

    def p_pass(first, count):
        def one(i, carry):
            target, up, edge = route(i)

            @pl.when((target != z) & (z != edge))
            def _():
                rcopy(i, up).wait_recv()
                pbuf[i] = (pbuf[i].astype(F32) + rin[up, i - 12].astype(F32)).astype(BF16)
                rcopy(i, up).start()

            return carry

        lax.fori_loop(first, first + count, one, 0)

    fresh(0, ysc, c2)
    e_start(0, 0)
    own.wait()
    staged[2].wait()
    x_part(0, 2)
    for r in range(1, SEQ):
        tcopy(r, peer(r)).wait_recv()
    e_wait(0, 0)
    scan_states(0, range(SEQ - 1, -1, -1))
    e_start(0, 1)
    w_wait(1, 0, 1)
    w_wait(1, 1, 1)
    x_part(2, 2)
    w_wait(2, 0, 2)
    go_send(2, 6, 0, 4)
    go_send(2, 3, 0, 1)
    w_wait(4, 1, 4)
    go_send(4, 6, 1, 2)
    go_send(4, 5, 1, 1)
    e_wait(0, 1)

    def back_finish(i, carry):
        cols = columns_of(i)
        state = rr[0, i // 2, pl.ds(pl.multiple_of((i % 2) * 128, 128), 128), :]
        pe = pexp[i]
        tail = jnp.exp(pe[SPAN - 1:SPAN, :] - pe)
        xg16[:, cols] = (xg[:, cols] + tail * dot_nt(b2[i // per_group], state)).astype(BF16)
        return carry

    lax.fori_loop(0, pairs, back_finish, 0)
    p_part(0, 4)
    w_wait(2, 1, 2)
    go_send(2, 3, 1, 1)
    w_wait(4, 0, 4)
    go_send(4, 5, 0, 1)
    x_part(4, 2)
    p_part(4, 2)
    x_part(8, 2)
    p_part(8, 2)
    for h in range(2):
        w_wait(3, h, 1)
        w_wait(5, h, 1)
    x_part(6, 2)
    p_part(6, 2)
    x_part(10, 2)
    p_part(10, 2)
    w_wait(6, 0, 4)
    go_send(6, 7, 0, 1)
    w_wait(6, 1, 2)
    go_send(6, 7, 1, 1)
    x_part(12, 2)
    p_part(12, 2)
    w_wait(7, 0, 1)
    w_wait(7, 1, 1)
    x_part(14, 2)

    def fore_scale(i, carry):
        cols = columns_of(i)
        x = xacc[:, cols].astype(BF16)
        x16[:, cols] = x
        pe = pexp[i]
        ysc[:, cols] = (x.astype(F32) * jnp.exp(pe[SPAN - 1:SPAN, :] - pe)).astype(BF16)
        return carry

    lax.fori_loop(0, pairs, fore_scale, 0)
    fresh(1, ysc, b2)
    e_start(1, 0)
    p_part(14, 2)
    p_pass(12, 2)
    e_wait(1, 0)
    scan_states(1, range(SEQ))
    e_start(1, 1)
    p_pass(14, 2)

    def fore_local(i, carry):
        cols = columns_of(i)
        x = x16[:, cols]
        y = jnp.where(left, dot_nn(wts[2 * i], x), dot_nn(wts[2 * i + 1], x))
        xacc[:, cols] = y + gain[i, 0:1, :] * x.astype(F32)
        return carry

    lax.fori_loop(0, pairs, fore_local, 0)
    e_wait(1, 1)

    def fore_finish(i, carry):
        cols = columns_of(i)
        state = rr[1, i // 2, pl.ds(pl.multiple_of((i % 2) * 128, 128), 128), :]
        y = xacc[:, cols] + jnp.exp(pexp[i]) * dot_nt(c2[i // per_group], state)
        gate = gz[:, cols].astype(F32)
        up = go[:, cols].astype(F32)
        sigma = jax.nn.sigmoid(gate)
        zg_ref[:, cols] = (up * y * sigma * (1.0 + gate * (1.0 - sigma))).astype(BF16)
        return carry

    lax.fori_loop(0, pairs, fore_finish, 0)

    def own_chunk(i, far):
        owner = peer_dyn(i // 2)

        @pl.when(owner // 2 == z)
        def _():
            piece = (owner % 2) * 2 + i % 2
            out_cols = pl.ds(pl.multiple_of(piece * 256, 256), 256)
            xg[:, out_cols] = pbuf[i].astype(F32)
            if far:
                @pl.when(z != 0)
                def _():
                    rcopy(i, 0).wait_recv()
                    xg[:, out_cols] += rin[0, i - 12].astype(F32)

                @pl.when(z != RUNS - 1)
                def _():
                    rcopy(i, 1).wait_recv()
                    xg[:, out_cols] += rin[1, i - 12].astype(F32)
            else:
                for dz in range(1, RUNS):
                    source = (z + dz) % RUNS
                    dcopy(i, source, source).wait_recv()
                    xg[:, out_cols] += rdir[source, i % 4].astype(F32)
            out_ref[:, out_cols] = xg[:, out_cols].astype(BF16)

    def own_near(i, carry):
        own_chunk(i, False)
        return carry

    def own_far(i, carry):
        own_chunk(i, True)
        return carry

    lax.fori_loop(0, 12, own_near, 0)
    lax.fori_loop(12, 16, own_far, 0)

    def drain(i, carry):
        target = route(i)[0]

        @pl.when(target != z)
        def _():
            dcopy(i, z, target).wait_send()

        return carry

    lax.fori_loop(0, 16, drain, 0)
    for cp in sent:
        cp.wait_send()
    for r in range(1, SEQ):
        tcopy(r, s).wait_send()
        for e in range(2):
            for f in range(2):
                ecopy(e, f, r, s).wait_send()


def fused_body(inputs, x_weight, b_values, c_values, gate_z, log_decay, skip_gain, grad_out):
    heads = log_decay.shape[1]
    width = x_weight.shape[1]
    depth = x_weight.shape[0]
    pairs = heads // 2
    groups = heads * GROUPS // HEADS
    b_flat = b_values.reshape(b_values.shape[0], GROUPS * STATE)
    c_flat = c_values.reshape(c_values.shape[0], GROUPS * STATE)
    halves = x_weight.reshape(2, depth // 2, width)
    vmem = pl.BlockSpec(memory_space=pltpu.VMEM)
    hbm = pl.BlockSpec(memory_space=pl.ANY)
    tokens = inputs.shape[0]
    dma = pltpu.SemaphoreType.DMA
    state = (2, SEQ, heads // SEQ * HEAD_DIM, STATE)
    return tuple(pl.pallas_call(
        mixer_kernel,
        out_shape=(
            jax.ShapeDtypeStruct((tokens, inputs.shape[1] // RUNS), BF16),
            jax.ShapeDtypeStruct((tokens, width), BF16),
        ),
        in_specs=[hbm, hbm, vmem, vmem, hbm, hbm, vmem, vmem],
        out_specs=(vmem, vmem),
        scratch_shapes=[
            pltpu.VMEM(inputs.shape, BF16),
            pltpu.VMEM((tokens, width), BF16),
            pltpu.VMEM((tokens, width), BF16),
            pltpu.VMEM((groups, SPAN, STATE), BF16),
            pltpu.VMEM((groups, SPAN, STATE), BF16),
            pltpu.VMEM((pairs, SPAN, 128), F32),
            pltpu.VMEM((pairs, 8, SPAN), F32),
            pltpu.VMEM((pairs, 8, 128), F32),
            pltpu.VMEM((SEQ, 8, 128), F32),
            pltpu.VMEM((SEQ, 2, depth // 2, width), BF16),
            pltpu.VMEM((tokens, width), F32),
            pltpu.VMEM((tokens, width), F32),
            pltpu.VMEM((tokens, width), BF16),
            pltpu.VMEM((tokens, width), BF16),
            pltpu.VMEM((heads, SPAN, SPAN), BF16),
            pltpu.VMEM((groups, SPAN, SPAN), F32),
            pltpu.VMEM((tokens, width), BF16),
            pltpu.VMEM((2 * SEQ, tokens, depth // 2), BF16),
            pltpu.VMEM((2, 4, tokens, depth // 2), BF16),
            pltpu.VMEM((RUNS, 4, tokens, depth // 2), BF16),
            pltpu.VMEM(state, BF16),
            pltpu.VMEM(state, BF16),
            pltpu.VMEM(state, BF16),
            pltpu.VMEM(state, BF16),
            pltpu.VMEM((SEQ, 8, 128), F32),
            dma((3,)), dma((SEQ, 2)), dma((SEQ, 2)), dma,
            dma((SEQ,)), dma((SEQ,)),
            dma((2, 2, SEQ)), dma((2, 2, SEQ)),
            dma((2 * SEQ,)), dma((2, 4)), dma((RUNS, 4)),
        ],
        compiler_params=pltpu.CompilerParams(
            collective_id=0, has_side_effects=True, vmem_limit_bytes=60 * 1024 * 1024),
        name="mixer",
    )(inputs, halves, b_flat, c_flat, gate_z, grad_out, log_decay, skip_gain[None, :]))


def solution(mesh):
    in_specs = (
        P("seq", None),
        P("seq", "head"),
        P("seq", None, None),
        P("seq", None, None),
        P("seq", "head"),
        P("seq", "head"),
        P("head"),
        P("seq", "head"),
    )
    out_specs = (P("seq", "head"), P("seq", "head"))
    small = mesh.shape["seq"] == SEQ and mesh.shape["head"] == RUNS
    chosen = fused_body if small else body
    return jax.shard_map(chosen, mesh=mesh, in_specs=in_specs, out_specs=out_specs, check_vma=False)
```
